128 devices in a mesh: src: 8 (over x, core), dst: 16 (over z, y).
Axes of the slice: x: 4, y: 4, z: 4, core: 2. Of those that a mesh axis runs over, the one named last changes fastest.
Arguments:
- edge_state: bfloat16 [262144, 512], P(('src', 'dst')), may hold values from -6 to 6
- directions: float32 [3, 262144], P(None, ('src', 'dst')), as said below
- src_atom: int32 [262144], P(('src', 'dst')), may hold values from 0 to 511
- dst_atom: int32 [262144], P(('src', 'dst')), may hold values from 0 to 255
- rev_pos: int32 [262144], P(('src', 'dst')), may hold values from 0 to 15, as said below
- counts: int32 [128, 128], P(('src', 'dst')), may hold values from 0 to 16, as said below
- triplets: int32 [2048, 4], P(('src', 'dst')), may hold values from 0 to 127
- down_w: bfloat16 [2, 512, 64], replicated, may hold values from -0.25 to 0.25
- trip_w: bfloat16 [2, 256, 512], replicated, may hold values from -0.75 to 0.75
- edge_w: bfloat16 [2, 6, 512, 512], replicated, may hold values from -0.25 to 0.25
Outputs:
- new_state: bfloat16 [262144, 512], P(('src', 'dst'))
The draws below stay inside these ranges and needn't reach their ends.
Inputs may be any that keep to these rules, and one draw needn't show every extreme that they name: `counts`: Symmetric, zero on the diagonal, and equal to 16 for some pair in every draw. Within each bucket b of device f, rev_pos maps the live positions one to one onto live positions of bucket f of device b, and the map for (b, f) is the inverse of that for (f, b); dead positions map to themselves. `directions`: unit vectors.
All inputs are finite; a program needn't handle non-finite values.
Results may differ from the reference program's by a relative error of at most 0.017.
Values may be sent and summed in bfloat16 or wider, within the bound.
A program may use at most 128 MiB of HBM per device.

```python
import math
import jax
import jax.numpy as jnp
from jax import lax

D = 512
TRIP = 64
NSPH = 4
BLK = 128
PAIRS = 4
NBLK = 2
EDGE_DEV = 2048
BUCKETS = 128
CAP = 16
EDGES = 262144
BLOCKS = 2048
ATOMS = 4096
DST_ATOMS = 256
SRC_ATOMS = 512
DEGREE = 64
N_SRC = 8
N_DST = 16


def pair_tables(key):
    key = jax.random.fold_in(key, 7)
    key_w, key_a, key_b, key_r = jax.random.split(key, 4)
    weights = jax.random.randint(key_w, (BUCKETS,), 1, 5)
    first = jax.random.randint(key_a, (), 0, BUCKETS)
    second = (first + 1 + jax.random.randint(key_b, (), 0, max(BUCKETS - 1, 1))) % BUCKETS
    weights = weights.at[first].set(4).at[second].set(4)
    rowid = jnp.arange(BUCKETS, dtype=jnp.int32)[:, None]
    colid = jnp.arange(BUCKETS, dtype=jnp.int32)[None, :]
    table = CAP * weights[:, None] * weights[None, :] // 16
    table = jnp.where(rowid == colid, 0, table).astype(jnp.int32)
    raw = jax.random.randint(key_r, (BUCKETS, BUCKETS, CAP), 0, 2 ** 20)
    lower = jnp.minimum(rowid, colid)
    upper = jnp.maximum(rowid, colid)
    shared = raw[lower, upper]
    slot = jnp.arange(CAP, dtype=jnp.int32)[None, None, :]
    keys = jnp.where(slot < table[:, :, None], shared * CAP + slot, 2 ** 20 * CAP + slot)
    order = jnp.argsort(keys, axis=-1, stable=True).astype(jnp.int32)
    inverse = jnp.argsort(order, axis=-1, stable=True).astype(jnp.int32)
    reverse = jnp.where((rowid < colid)[:, :, None], order, inverse).astype(jnp.int32)
    return (table, reverse.reshape(-1))


def draw_counts(key, part):
    return pair_tables(key)[0]


def draw_rev_pos(key, part):
    return pair_tables(key)[1]


def draw_directions(key, part):
    key = jax.random.fold_in(key, 11)
    key_z, key_p = jax.random.split(key)
    total = BUCKETS * EDGE_DEV
    height = jax.random.uniform(key_z, (total,), jnp.float32, -1.0, 1.0)
    angle = jax.random.uniform(key_p, (total,), jnp.float32, -math.pi, math.pi)
    radius = jnp.sqrt(jnp.maximum(1.0 - height * height, 0.0))
    return jnp.stack([radius * jnp.cos(angle), radius * jnp.sin(angle), height]).astype(jnp.float32)


def set_ends(result, key, smallest, largest):
    place = [jax.random.randint(jax.random.fold_in(key, axis), (), 0, length) for axis, length in enumerate(result.shape)]
    longest = result.shape.index(max(result.shape))
    neighbour = place[:longest] + [(place[longest] + 1) % result.shape[longest]] + place[longest + 1:]
    return result.at[tuple(place)].set(smallest).at[tuple(neighbour)].set(largest)


def levels(own_key, extent, cuts, low, high):
    gain, own = 1.0, jax.random.fold_in(own_key, 6)
    for dim, parts in cuts:
        draws = jnp.exp(jax.random.uniform(jax.random.fold_in(own, dim), (parts,), jnp.float32, low / len(cuts), high / len(cuts)))
        gain = gain * jnp.repeat(draws, extent[dim] // parts).reshape([-1 if axis == dim else 1 for axis in range(len(extent))])
    return gain


def noise(own_key, shape, width, limit, shards=(), kind=jnp.bfloat16):
    entries = jax.random.normal(own_key, shape, jnp.float32) * width
    if len(shards) > 0:
        entries = levels(own_key, shape, shards, -0.22, 0.18) * entries
    return jnp.clip(entries, min=-limit, max=limit).astype(kind)


def setup_inputs(seed: int = 0) -> dict:
    key_of = jax.random.split(jax.random.key(seed), 11)
    return {
        "edge_state": noise(key_of[0], (EDGES, D), 1.0, 6.0, ((0, 128),)),
        "directions": draw_directions(jax.random.fold_in(key_of[10], 71), 0),
        "src_atom": set_ends(jax.random.randint(key_of[2], (EDGES,), 0, SRC_ATOMS), jax.random.fold_in(key_of[2], 1), 0, SRC_ATOMS - 1).astype(jnp.int32),
        "dst_atom": set_ends(jax.random.randint(key_of[3], (EDGES,), 0, DST_ATOMS), jax.random.fold_in(key_of[3], 1), 0, DST_ATOMS - 1).astype(jnp.int32),
        "rev_pos": draw_rev_pos(jax.random.fold_in(key_of[10], 71), 0),
        "counts": draw_counts(jax.random.fold_in(key_of[10], 71), 0),
        "triplets": set_ends(jax.random.randint(key_of[6], (BLOCKS, PAIRS), 0, N_SRC * EDGE_DEV // BLK), jax.random.fold_in(key_of[6], 1), 0, (N_SRC * EDGE_DEV // BLK) - 1).astype(jnp.int32),
        "down_w": noise(key_of[7], (NBLK, D, TRIP), D ** -0.5, 0.25),
        "trip_w": noise(key_of[8], (NBLK, NSPH * TRIP, D), TRIP ** -0.5, 0.75),
        "edge_w": noise(key_of[9], (NBLK, 6, D, D), D ** -0.5, 0.25),
    }


def legendre(cosine):
    square = cosine * cosine
    return [cosine, 1.5 * square - 0.5, 2.5 * square * cosine - 1.5 * cosine, (35.0 * square * square - 30.0 * square + 3.0) / 8.0]


def silu(value):
    return value / (1.0 + jnp.exp(-value))


def reference(edge_state, directions, src_atom, dst_atom, rev_pos, counts, triplets, down_w, trip_w, edge_w):
    nblock = EDGE_DEV // BLK
    live = (jnp.arange(CAP)[None, None, :] < counts[:, :, None]).reshape(EDGES)
    live_f = live.astype(jnp.float32)[:, None]
    dirs_dev = directions.reshape(3, BUCKETS, nblock, BLK)
    dirs_grid = directions.reshape(3, N_SRC, N_DST, nblock, BLK)
    trip_dev = triplets.reshape(BUCKETS, nblock, PAIRS)
    tri_scale = (BLK * PAIRS) ** -0.5
    slot_dev = jnp.arange(EDGES, dtype=jnp.int32) // EDGE_DEV
    dst_id = (slot_dev % N_DST) * DST_ATOMS + dst_atom
    src_id = (slot_dev // N_DST) * SRC_ATOMS + src_atom
    state = edge_state
    for level in range(NBLK):
        lowered = (silu(jnp.dot(state, down_w[level], preferred_element_type=jnp.float32)) * live_f).astype(jnp.bfloat16)
        low_grid = lowered.reshape(N_SRC, N_DST, nblock, BLK, TRIP)

        def triple_for(flat):
            column = flat % N_DST
            local = dirs_dev[:, flat]
            pool_dirs = dirs_grid[:, :, column].reshape(3, N_SRC * nblock, BLK)
            chosen_dirs = pool_dirs[:, trip_dev[flat]]
            cosine = jnp.einsum("cbk,cbqm->bqkm", local, chosen_dirs, precision=lax.Precision.HIGHEST)
            tiles = jnp.stack(legendre(cosine)).astype(jnp.bfloat16)
            pool = low_grid[:, column].reshape(N_SRC * nblock, BLK, TRIP)
            chosen = pool[trip_dev[flat]]
            summed = jnp.einsum("lbqkm,bqmt->bklt", tiles.astype(jnp.float32), chosen.astype(jnp.float32))
            return (summed * tri_scale).reshape(EDGE_DEV, NSPH * TRIP).astype(jnp.bfloat16)

        triple = lax.map(triple_for, jnp.arange(BUCKETS, dtype=jnp.int32)).reshape(EDGES, NSPH * TRIP)
        layer_w = edge_w[level]
        pre = jnp.dot(state, layer_w[0], preferred_element_type=jnp.float32) + jnp.dot(triple, trip_w[level], preferred_element_type=jnp.float32)
        message = (silu(pre) * live_f).astype(jnp.bfloat16)
        swapped = message.reshape(BUCKETS, BUCKETS, CAP, D).transpose(1, 0, 2, 3)
        mirrored = jnp.take_along_axis(swapped, rev_pos.reshape(BUCKETS, BUCKETS, CAP, 1), axis=2).reshape(EDGES, D)
        symmetric = (message.astype(jnp.float32) + mirrored.astype(jnp.float32) * live_f).astype(jnp.bfloat16)
        inner = silu(jnp.dot(symmetric, layer_w[1], preferred_element_type=jnp.float32)).astype(jnp.bfloat16)
        refined = (symmetric.astype(jnp.float32) + jnp.dot(inner, layer_w[2], preferred_element_type=jnp.float32)).astype(jnp.bfloat16)
        totals = jax.ops.segment_sum(refined.astype(jnp.float32), dst_id, num_segments=ATOMS)
        atoms = (totals * (DEGREE ** -0.5)).astype(jnp.bfloat16)
        feed = atoms[src_id]
        joined = (refined.astype(jnp.float32) + feed.astype(jnp.float32)).astype(jnp.bfloat16)
        first = silu(jnp.dot(joined, layer_w[3], preferred_element_type=jnp.float32)).astype(jnp.bfloat16)
        second = silu(jnp.dot(first, layer_w[4], preferred_element_type=jnp.float32)).astype(jnp.bfloat16)
        update = state.astype(jnp.float32) + refined.astype(jnp.float32) + jnp.dot(second, layer_w[5], preferred_element_type=jnp.float32)
        state = (update * live_f * (0.5 ** 0.5)).astype(jnp.bfloat16)
    return state
```

```python
import jax
import jax.numpy as jnp
from jax import lax
from jax.sharding import PartitionSpec as P

BLK = 128
PAIRS = 4
NBLK = 2
ATOM_DEV = 32
DEGREE = 64


def copy_for_each(array, axis):
    length = lax.axis_size(axis)
    return lax.all_to_all(
        jnp.broadcast_to(array[None], (length, *array.shape)), axis, 0, 0, tiled=True
    )


def laid_out(tiles, dim):
    tiles = jnp.moveaxis(tiles, 0, dim)
    lengths = tiles.shape
    return tiles.reshape(*lengths[:dim], lengths[dim] * lengths[dim + 1], *lengths[dim + 2 :])


def collect(array, axis, dim):
    tiles = copy_for_each(array, axis)
    return laid_out(tiles, dim)


def region_atoms(partial_sums):
    n_src = lax.axis_size("src")
    n_dst = lax.axis_size("dst")
    group = n_dst // n_src
    rows, width = partial_sums.shape
    pieces = partial_sums.astype(jnp.bfloat16).reshape(n_src, rows // n_src, width)
    pieces = lax.all_to_all(pieces, "src", 0, 0, tiled=True)
    atoms = (pieces.astype(jnp.float32).sum(0) * DEGREE ** (-0.5)).astype(jnp.bfloat16)
    moves = [
        (s * n_dst + d, (d // group) * n_dst + s * group + d % group)
        for s in range(n_src)
        for d in range(n_dst)
    ]
    atoms = lax.ppermute(atoms, ("src", "dst"), moves)
    region = lax.all_gather(atoms, "dst", axis=0)
    region = region.reshape(n_src, group, rows // n_src, width)
    return jnp.moveaxis(region, 1, 0).reshape(group * rows, width)


def legendre(cosine):
    square = cosine * cosine
    return [
        cosine,
        1.5 * square - 0.5,
        2.5 * square * cosine - 1.5 * cosine,
        (35.0 * square * square - 30.0 * square + 3.0) / 8.0,
    ]


def silu(value):
    return value / (1.0 + jnp.exp(-value))


def body(
    edge_state, directions, src_atom, dst_atom, rev_pos, counts, triplets, down_w, trip_w, edge_w
):
    n_src = lax.axis_size("src")
    n_dst = lax.axis_size("dst")
    rows, width = edge_state.shape
    buckets = counts.shape[1]
    bucket_cap = rows // buckets
    nblock = rows // BLK
    live = (jnp.arange(bucket_cap)[None, :] < counts[0][:, None]).reshape(rows, 1)
    live_f = live.astype(jnp.float32)
    pool_dirs = collect(directions, "src", 1)
    chosen_dirs = jnp.take(pool_dirs.reshape(3, n_src * nblock, BLK), triplets, axis=1)
    local_dirs = directions.reshape(3, nblock, BLK)
    cosine = jnp.einsum("cbk,cbqm->bqkm", local_dirs, chosen_dirs, precision=lax.Precision.HIGHEST)
    tiles = jnp.stack(legendre(cosine)).astype(jnp.bfloat16)
    tri_scale = (BLK * PAIRS) ** (-0.5)
    dst_rows = ATOM_DEV * n_src
    group = n_dst // n_src
    onehot = (dst_atom[:, None] == jnp.arange(dst_rows, dtype=jnp.int32)[None, :]).astype(
        jnp.bfloat16
    )
    pick = (
        src_atom[:, None] == jnp.arange(group * dst_rows, dtype=jnp.int32)[None, :]
    ).astype(jnp.bfloat16)
    slot = jnp.arange(rows, dtype=jnp.int32) % BLK
    target = (slot - slot % bucket_cap + rev_pos).reshape(nblock, BLK, 1)
    mirror = (target == jnp.arange(BLK, dtype=jnp.int32)).astype(jnp.bfloat16)
    state = edge_state
    for level in range(NBLK):
        layer_w = edge_w[level]
        lowered = (
            silu(jnp.dot(state, down_w[level], preferred_element_type=jnp.float32)) * live_f
        ).astype(jnp.bfloat16)
        pooled = collect(lowered.reshape(-1, 128), "src", 0).reshape(n_src * nblock, BLK, -1)
        chosen = jnp.take(pooled, triplets, axis=0)
        summed = jnp.einsum("lbqkm,bqmt->bklt", tiles, chosen, preferred_element_type=jnp.float32)
        triple = (summed * tri_scale).reshape(rows, -1).astype(jnp.bfloat16)
        pre = jnp.dot(state, layer_w[0], preferred_element_type=jnp.float32) + jnp.dot(
            triple, trip_w[level], preferred_element_type=jnp.float32
        )
        message = (silu(pre) * live_f).astype(jnp.bfloat16)
        arrived = lax.all_to_all(
            message.reshape(buckets, bucket_cap, width),
            ("src", "dst"),
            split_axis=0,
            concat_axis=0,
            tiled=True,
        )
        mirrored = jnp.einsum(
            "cij,cjd->cid",
            mirror,
            arrived.reshape(nblock, BLK, width),
            preferred_element_type=jnp.float32,
        ).reshape(rows, width)
        symmetric = (message.astype(jnp.float32) + mirrored * live_f).astype(
            jnp.bfloat16
        )
        inner = silu(jnp.dot(symmetric, layer_w[1], preferred_element_type=jnp.float32)).astype(
            jnp.bfloat16
        )
        refined = (
            symmetric.astype(jnp.float32)
            + jnp.dot(inner, layer_w[2], preferred_element_type=jnp.float32)
        ).astype(jnp.bfloat16)
        partial_sums = jnp.einsum("ea,ed->ad", onehot, refined, preferred_element_type=jnp.float32)
        region = region_atoms(partial_sums)
        feed = jnp.dot(pick, region, preferred_element_type=jnp.float32)
        joined = (refined.astype(jnp.float32) + feed).astype(jnp.bfloat16)
        first = silu(jnp.dot(joined, layer_w[3], preferred_element_type=jnp.float32)).astype(
            jnp.bfloat16
        )
        second = silu(jnp.dot(first, layer_w[4], preferred_element_type=jnp.float32)).astype(
            jnp.bfloat16
        )
        update = (
            state.astype(jnp.float32)
            + refined.astype(jnp.float32)
            + jnp.dot(second, layer_w[5], preferred_element_type=jnp.float32)
        )
        state = (update * live_f * 0.5**0.5).astype(jnp.bfloat16)
    return state


def solution(mesh):
    placed = (
        P(("src", "dst"), None),
        P(None, ("src", "dst")),
        P(("src", "dst")),
        P(("src", "dst")),
        P(("src", "dst")),
        P(("src", "dst"), None),
        P(("src", "dst"), None),
        P(),
        P(),
        P(),
    )
    return jax.shard_map(
        body, mesh=mesh, in_specs=placed, out_specs=P(("src", "dst"), None), check_vma=False
    )
```

```python
import jax
import jax.numpy as jnp
from jax import lax
from jax.experimental import pallas as pl
from jax.experimental.pallas import tpu as pltpu
from jax.sharding import PartitionSpec as P

BLK = 128
PAIRS = 4
NBLK = 2
NSPH = 4
TRIP = 64
DEGREE = 64
N_SRC = 8
N_DST = 16
DEVS = N_SRC * N_DST
CAP = 16
WIDTH = 512
ROWS = DEVS * CAP
CHUNK = N_DST * CAP
NBLOCK = ROWS // BLK
BPC = CHUNK // BLK
ATOM_ROWS = 256
PIECE = ATOM_ROWS // N_SRC
MESH = pl.DeviceIdType.MESH
F32 = jnp.float32
BF16 = jnp.bfloat16


def silu(value):
    half = 0.5 * value
    return half + half * jnp.tanh(half)


def dot(a, b):
    return jnp.dot(a, b, preferred_element_type=F32)


def loop(count, step):
    def body(i, carry):
        step(i)
        return carry

    lax.fori_loop(0, count, body, 0)


def kernel(
    tri,
    col,
    dirs_in,
    state_in,
    onehot_in,
    mirror_in,
    pick_in,
    down_in,
    trip_in,
    edge_in,
    out,
    state,
    base,
    msg,
    arr,
    refined,
    tiles,
    pool,
    dirs,
    onehot,
    mirror,
    pick,
    down,
    trip,
    edge,
    total,
    part,
    gathered,
    atoms,
    region,
    load_sem,
    out_sem,
    dirs_send,
    dirs_recv,
    pool_send,
    pool_recv,
    side_send,
    side_recv,
    msg_send,
    msg_recv,
    part_send,
    part_recv,
    atom_send,
    atom_recv,
):
    s = lax.axis_index("src")
    d = lax.axis_index("dst")
    me = s * N_DST + d
    x = s // 2
    core = s % 2
    twin = x * 2 + (1 - core)

    def remote(src, dst, send, recv, ts, td):
        return pltpu.make_async_remote_copy(
            src_ref=src,
            dst_ref=dst,
            send_sem=send,
            recv_sem=recv,
            device_id=(ts, td),
            device_id_type=MESH,
        )

    def drain(ref, sem):
        pltpu.make_async_copy(ref, ref, sem).wait()

    barrier = pltpu.get_barrier_semaphore()

    def greet(i):
        t = (me + 1 + i) % DEVS
        pl.semaphore_signal(
            barrier, inc=1, device_id=(t // N_DST, t % N_DST), device_id_type=MESH
        )

    loop(DEVS - 1, greet)
    loads = [
        pltpu.make_async_copy(a, b, load_sem.at[i])
        for i, (a, b) in enumerate(
            [
                (state_in, state),
                (down_in, down),
                (dirs_in, dirs.at[s]),
                (edge_in, edge),
                (trip_in, trip),
                (mirror_in, mirror),
                (onehot_in, onehot),
                (pick_in, pick),
            ]
        )
    ]
    for load in loads:
        load.start()
    total[...] = jnp.zeros_like(total)
    arr[pl.ds(me, 1)] = jnp.zeros((1, CAP, WIDTH), BF16)

    def rows_of(ref, g):
        return ref[pl.ds(g * N_DST, N_DST)].reshape(CHUNK, WIDTH)

    def put_rows(ref, g, value):
        ref[pl.ds(g * N_DST, N_DST)] = value.reshape(N_DST, CAP, WIDTH)

    def live_of(g):
        return col[pl.ds(pl.multiple_of(g * CHUNK, CHUNK), CHUNK), 3:4]

    def lower(level, g, value):
        low = (silu(dot(value, down[level])) * live_of(g)).astype(BF16)
        low = low.reshape(BPC, 2, BLK // 2, TRIP)
        pool[pl.ds(s * NBLOCK + g * BPC, BPC)] = jnp.concatenate(
            [low[:, 0], low[:, 1]], axis=-1
        )

    def share(g, k):
        piece = pool.at[pl.ds(s * NBLOCK + g * BPC, BPC)]
        for hop in range(1, 4):
            remote(
                piece,
                piece,
                pool_send.at[hop - 1, k],
                pool_recv.at[s, k],
                ((x + hop) % 4) * 2 + core,
                d,
            ).start()
        remote(piece, piece, side_send.at[0, k], side_recv.at[x, k], twin, d).start()

    def forward(k):
        for hop in range(1, 4):
            owner = ((x + 4 - hop) % 4) * 2 + core
            piece = pool.at[pl.ds(owner * NBLOCK + k * BPC, BPC)]
            drain(piece, pool_recv.at[owner, k])
            remote(
                piece, piece, side_send.at[hop, k], side_recv.at[owner // 2, k], twin, d
            ).start()

    def settle(k):
        for hop in range(4):
            owner = ((x + hop) % 4) * 2 + (1 - core)
            piece = pool.at[pl.ds(owner * NBLOCK + k * BPC, BPC)]
            drain(piece, side_recv.at[owner // 2, k])
            drain(piece, side_send.at[hop, k])
        for hop in range(3):
            drain(piece, pool_send.at[hop, k])

    def base_of(level, g):
        base[pl.ds(pl.multiple_of(g * CHUNK, CHUNK), CHUNK), :] = dot(
            rows_of(state, g), edge[level, 0]
        )

    loads[0].wait()
    loads[1].wait()
    loads[2].wait()
    loop(N_SRC, lambda g: lower(0, g, rows_of(state, g)))
    pl.semaphore_wait(barrier, DEVS - 1)
    for hop in range(1, N_SRC):
        remote(
            dirs.at[s],
            dirs.at[s],
            dirs_send.at[hop],
            dirs_recv.at[s],
            (s + hop) % N_SRC,
            d,
        ).start()
    loop(N_SRC, lambda g: share(g, g))
    loads[3].wait()
    loop(N_SRC, lambda g: base_of(0, g))
    for load in loads[4:]:
        load.wait()
    for hop in range(1, N_SRC):
        drain(dirs.at[s], dirs_send.at[hop])
        owner = (s + hop) % N_SRC
        drain(dirs.at[owner], dirs_recv.at[owner])

    def angles(c):
        start = pl.multiple_of(c * BLK, BLK)
        mine = [
            jnp.broadcast_to(col[pl.ds(start, BLK), i : i + 1], (BLK, BLK)) for i in range(3)
        ]
        for q in range(PAIRS):
            pick_block = tri[c, q]
            other = dirs[pick_block // NBLOCK, pick_block % NBLOCK]
            cosine = mine[0] * other[0:1, :] + mine[1] * other[1:2, :] + mine[2] * other[2:3, :]
            square = cosine * cosine
            values = [
                cosine,
                1.5 * square - 0.5,
                (2.5 * square - 1.5) * cosine,
                (35.0 * square * square - 30.0 * square + 3.0) * 0.125,
            ]
            for i, value in enumerate(values):
                tiles[c, i * BLK : (i + 1) * BLK, q * BLK : (q + 1) * BLK] = value.astype(BF16)

    loop(NBLOCK, angles)

    def run_level(level):
        loop(N_SRC, forward)
        loop(N_SRC, settle)

        def talk(j):
            g = (s + 1 + j) % N_SRC
            parts = []
            for i in range(BPC):
                c = g * BPC + i
                chosen = []
                for q in range(PAIRS):
                    block = pool[tri[c, q]]
                    chosen += [block[:, :TRIP], block[:, TRIP:]]
                summed = dot(tiles[c], jnp.concatenate(chosen, axis=0))
                summed = (summed * (BLK * PAIRS) ** (-0.5)).astype(BF16)
                parts.append(
                    jnp.concatenate(
                        [summed[n * BLK : (n + 1) * BLK] for n in range(NSPH)], axis=1
                    )
                )
            triple = jnp.concatenate(parts, axis=0)
            pre = base[pl.ds(pl.multiple_of(g * CHUNK, CHUNK), CHUNK), :] + dot(
                triple, trip[level]
            )
            put_rows(msg, g, (silu(pre) * live_of(g)).astype(BF16))

            def send(i):
                t = (d + 1 + i) % N_DST
                b = g * N_DST + t

                @pl.when(b != me)
                def _():
                    remote(msg.at[b], arr.at[me], msg_send, msg_recv.at[s], g, t).start()

            loop(N_DST, send)

        loop(N_SRC, talk)

        def listen(j):
            g = (s + N_SRC - 1 - j) % N_SRC

            @pl.when(g != s)
            def _():
                drain(arr.at[pl.ds(g * N_DST, N_DST)], msg_recv.at[g])

            @pl.when(g == s)
            def _():
                drain(arr.at[pl.ds(0, N_DST - 1)], msg_recv.at[g])

            came = rows_of(arr, g)
            mirrored = jnp.concatenate(
                [
                    dot(mirror[g * BPC + i], came[i * BLK : (i + 1) * BLK])
                    for i in range(BPC)
                ],
                axis=0,
            )
            symmetric = (rows_of(msg, g).astype(F32) + mirrored).astype(BF16)
            inner = silu(dot(symmetric, edge[level, 1])).astype(BF16)
            value = (symmetric.astype(F32) + dot(inner, edge[level, 2])).astype(BF16)
            put_rows(refined, g, value)
            total[...] += dot(onehot[g], value)

        loop(N_SRC, listen)
        part[...] = total[...].astype(BF16).reshape(N_SRC, PIECE, WIDTH)
        for hop in range(1, N_SRC):
            t = (s + hop) % N_SRC
            remote(part.at[t], gathered.at[s], part_send.at[hop], part_recv.at[s], t, d).start()
        gathered[pl.ds(s, 1)] = part[pl.ds(s, 1)]
        total[...] = jnp.zeros_like(total)
        drain(arr.at[pl.ds(0, DEVS - 1)], msg_send)
        for hop in range(1, N_SRC):
            owner = (s + hop) % N_SRC
            drain(gathered.at[owner], part_recv.at[owner])
        sums = gathered[0].astype(F32)
        for i in range(1, N_SRC):
            sums += gathered[i].astype(F32)
        sums = (sums * DEGREE ** (-0.5)).astype(BF16)
        atoms[...] = sums
        home = d // 2
        slot = d % 2

        def spread(i):
            t = (d + 1 + i) % N_DST

            @pl.when(home * N_DST + t != me)
            def _():
                remote(
                    atoms, region.at[slot, s], atom_send, atom_recv, home, t
                ).start()

        loop(N_DST, spread)

        @pl.when(home == s)
        def _():
            region[pl.ds(slot, 1), pl.ds(s, 1)] = sums[None, None]
            drain(arr.at[pl.ds(0, 2 * (N_DST - 1))], atom_recv)
            drain(arr.at[pl.ds(0, 2 * (N_DST - 1))], atom_send)

        @pl.when(home != s)
        def _():
            drain(arr.at[pl.ds(0, 2 * N_DST)], atom_recv)
            drain(arr.at[pl.ds(0, 2 * N_DST)], atom_send)

        for hop in range(1, N_SRC):
            drain(part.at[0], part_send.at[hop])

        def update(g):
            value = rows_of(refined, g).astype(F32)
            feed = dot(pick[g], region[...].reshape(2 * ATOM_ROWS, WIDTH))
            joined = (value + feed).astype(BF16)
            first = silu(dot(joined, edge[level, 3])).astype(BF16)
            second = silu(dot(first, edge[level, 4])).astype(BF16)
            fresh = rows_of(state, g).astype(F32) + value + dot(second, edge[level, 5])
            fresh = (fresh * (live_of(g) * 0.5**0.5)).astype(BF16)
            put_rows(state, g, fresh)

            @pl.when(level < NBLK - 1)
            def _():
                lower(level + 1, g, fresh)
                share(g, g)

            @pl.when(level == NBLK - 1)
            def _():
                piece = pl.ds(g * N_DST, N_DST)
                pltpu.make_async_copy(state.at[piece], out.at[piece], out_sem).start()

        loop(N_SRC, update)

        @pl.when(level < NBLK - 1)
        def _():
            loop(N_SRC, lambda g: base_of(level + 1, g))

    loop(NBLK, run_level)
    drain(state, out_sem)


def body(
    edge_state, directions, src_atom, dst_atom, rev_pos, counts, triplets, down_w, trip_w, edge_w
):
    live = (jnp.arange(CAP)[None, :] < counts[0][:, None]).reshape(ROWS, 1)
    col = jnp.concatenate([directions.T, live.astype(F32)], axis=1)
    dirs = jnp.moveaxis(directions.reshape(3, NBLOCK, BLK), 0, 1)
    onehot = (
        dst_atom.reshape(N_SRC, 1, CHUNK) == jnp.arange(ATOM_ROWS, dtype=jnp.int32)[:, None]
    ).astype(BF16)
    slot = jnp.arange(ROWS, dtype=jnp.int32) % BLK
    target = (slot - slot % CAP + rev_pos).reshape(NBLOCK, BLK, 1)
    mirror = (
        (target == jnp.arange(BLK, dtype=jnp.int32)) & live.reshape(NBLOCK, BLK, 1)
    ).astype(BF16)
    pick = (
        src_atom.reshape(N_SRC, CHUNK, 1) == jnp.arange(2 * ATOM_ROWS, dtype=jnp.int32)
    ).astype(BF16)
    vmem = pl.BlockSpec(memory_space=pltpu.VMEM)
    hbm = pl.BlockSpec(memory_space=pl.ANY)
    dma = pltpu.SemaphoreType.DMA
    out = pl.pallas_call(
        kernel,
        out_shape=jax.ShapeDtypeStruct((DEVS, CAP, WIDTH), BF16),
        in_specs=[pl.BlockSpec(memory_space=pltpu.SMEM), vmem] + [hbm] * 8,
        out_specs=hbm,
        scratch_shapes=[
            pltpu.VMEM((DEVS, CAP, WIDTH), BF16),
            pltpu.VMEM((ROWS, WIDTH), F32),
            pltpu.VMEM((DEVS, CAP, WIDTH), BF16),
            pltpu.VMEM((DEVS, CAP, WIDTH), BF16),
            pltpu.VMEM((DEVS, CAP, WIDTH), BF16),
            pltpu.VMEM((NBLOCK, NSPH * BLK, PAIRS * BLK), BF16),
            pltpu.VMEM((N_SRC * NBLOCK, BLK // 2, 2 * TRIP), BF16),
            pltpu.VMEM((N_SRC, NBLOCK, 3, BLK), F32),
            pltpu.VMEM(onehot.shape, BF16),
            pltpu.VMEM(mirror.shape, BF16),
            pltpu.VMEM(pick.shape, BF16),
            pltpu.VMEM(down_w.shape, BF16),
            pltpu.VMEM(trip_w.shape, BF16),
            pltpu.VMEM(edge_w.shape, BF16),
            pltpu.VMEM((ATOM_ROWS, WIDTH), F32),
            pltpu.VMEM((N_SRC, PIECE, WIDTH), BF16),
            pltpu.VMEM((N_SRC, PIECE, WIDTH), BF16),
            pltpu.VMEM((PIECE, WIDTH), BF16),
            pltpu.VMEM((2, N_SRC, PIECE, WIDTH), BF16),
            dma((8,)),
            dma,
            dma((N_SRC,)),
            dma((N_SRC,)),
            dma((3, N_SRC)),
            dma((N_SRC, N_SRC)),
            dma((4, N_SRC)),
            dma((4, N_SRC)),
            dma,
            dma((N_SRC,)),
            dma((N_SRC,)),
            dma((N_SRC,)),
            dma,
            dma,
        ],
        compiler_params=pltpu.CompilerParams(
            collective_id=0, has_side_effects=True, vmem_limit_bytes=60 << 20
        ),
    )(
        triplets,
        col,
        dirs,
        edge_state.reshape(DEVS, CAP, WIDTH),
        onehot,
        mirror,
        pick,
        down_w,
        trip_w,
        edge_w,
    )
    return out.reshape(ROWS, WIDTH)


def solution(mesh):
    placed = (
        P(("src", "dst"), None),
        P(None, ("src", "dst")),
        P(("src", "dst")),
        P(("src", "dst")),
        P(("src", "dst")),
        P(("src", "dst"), None),
        P(("src", "dst"), None),
        P(),
        P(),
        P(),
    )
    return jax.shard_map(
        body, mesh=mesh, in_specs=placed, out_specs=P(("src", "dst"), None), check_vma=False
    )
```

```python
import jax
import jax.numpy as jnp
from jax import lax
from jax.experimental import pallas as pl
from jax.experimental.pallas import tpu as pltpu
from jax.sharding import PartitionSpec as P

BLK = 128
PAIRS = 4
NBLK = 2
HARM = 24
HPAD = 32
TRIP = 64
DEGREE = 64
N_SRC = 8
N_DST = 16
DEVS = N_SRC * N_DST
CAP = 16
WIDTH = 512
ROWS = DEVS * CAP
CHUNK = N_DST * CAP
NBLOCK = ROWS // BLK
BPC = CHUNK // BLK
ATOM_ROWS = 256
PIECE = ATOM_ROWS // N_SRC
MESH = pl.DeviceIdType.MESH
F32 = jnp.float32
BF16 = jnp.bfloat16


def silu(value):
    half = 0.5 * value
    return half + half * jnp.tanh(half)


def dot(a, b):
    return jnp.dot(a, b, preferred_element_type=F32)


def loop(count, step):
    def body(i, carry):
        step(i)
        return carry

    lax.fori_loop(0, count, body, 0)


def harmonics(x, y, z):
    xx, yy, zz = x * x, y * y, z * z
    diff = xx - yy
    r3, r5, r15, r35 = 3.0**0.5, 5.0**0.5, 15.0**0.5, 35.0**0.5
    r38, r58, r358 = 0.375**0.5, 0.625**0.5, 4.375**0.5
    return [
        x,
        y,
        z,
        r3 * x * y,
        r3 * y * z,
        r3 * x * z,
        0.5 * r3 * diff,
        1.5 * zz - 0.5,
        r58 * y * (3.0 * xx - yy),
        r15 * x * y * z,
        r38 * y * (5.0 * zz - 1.0),
        0.5 * z * (5.0 * zz - 3.0),
        r38 * x * (5.0 * zz - 1.0),
        0.5 * r15 * z * diff,
        r58 * x * (xx - 3.0 * yy),
        0.5 * r35 * x * y * diff,
        r358 * y * z * (3.0 * xx - yy),
        0.5 * r5 * x * y * (7.0 * zz - 1.0),
        r58 * y * z * (7.0 * zz - 3.0),
        0.125 * (35.0 * zz * zz - 30.0 * zz + 3.0),
        r58 * x * z * (7.0 * zz - 3.0),
        0.25 * r5 * diff * (7.0 * zz - 1.0),
        r358 * x * z * (xx - 3.0 * yy),
        0.125 * r35 * (xx * xx - 6.0 * xx * yy + yy * yy),
    ]


def kernel(
    tri,
    dirs_in,
    src_in,
    dst_in,
    rev_in,
    counts_in,
    state_in,
    down_in,
    trip_in,
    edge_in,
    out,
    state,
    base,
    msg,
    arr,
    refined,
    split,
    field,
    rows_y,
    cols,
    pool,
    spectrum,
    lifted,
    onehot,
    mirror,
    pick,
    down,
    trip,
    edge,
    total,
    part,
    gathered,
    atoms,
    region,
    load_sem,
    out_sem,
    pool_send,
    pool_recv,
    msg_send,
    msg_recv,
    part_send,
    part_recv,
    atom_send,
    atom_recv,
):
    s = lax.axis_index("src")
    d = lax.axis_index("dst")
    me = s * N_DST + d
    x = s // 2
    z = d // 4
    y = d % 4

    def remote(src, dst, send, recv, ts, td):
        return pltpu.make_async_remote_copy(
            src_ref=src,
            dst_ref=dst,
            send_sem=send,
            recv_sem=recv,
            device_id=(ts, td),
            device_id_type=MESH,
        )

    def drain(ref, sem):
        pltpu.make_async_copy(ref, ref, sem).wait()

    barrier = pltpu.get_barrier_semaphore()

    def greet(i):
        t = (me + 1 + i) % DEVS
        pl.semaphore_signal(
            barrier, inc=1, device_id=(t // N_DST, t % N_DST), device_id_type=MESH
        )

    loop(DEVS - 1, greet)
    loads = [
        pltpu.make_async_copy(a, b, load_sem.at[i])
        for i, (a, b) in enumerate(
            [(state_in, state), (down_in, down), (edge_in, edge), (trip_in, trip)]
        )
    ]
    for load in loads:
        load.start()
    total[...] = jnp.zeros_like(total)
    arr[pl.ds(me, 1)] = jnp.zeros((1, CAP, WIDTH), BF16)

    def iota(shape, axis):
        return lax.broadcasted_iota(jnp.int32, shape, axis)

    lane = iota((NBLOCK, BLK), 1)
    number = iota((NBLOCK, BLK), 0)
    spread_counts = jnp.where(
        lane // (BLK // CAP) == number,
        jnp.broadcast_to(counts_in[...], (NBLOCK, BLK)),
        0,
    ).astype(F32)
    widen = iota((BLK, BLK), 0) % (BLK // CAP) == iota((BLK, BLK), 1) // CAP
    filled = dot(spread_counts.astype(BF16), widen.astype(F32).astype(BF16))
    slot = lane % CAP
    for c in range(NBLOCK):
        split[c, 0:3, :] = dirs_in[:, c * BLK : (c + 1) * BLK]
    field[...] = jnp.zeros_like(field)
    planes = harmonics(split[:, 0, :], split[:, 1, :], split[:, 2, :])
    for i, plane in enumerate(planes):
        field[:, i, :] = plane
    rows_y[...] = field[...].astype(BF16)
    field[:, HARM, :] = (slot.astype(F32) < filled).astype(F32)
    field[:, HARM + 1, :] = src_in[...].astype(F32)
    field[:, HARM + 2, :] = (lane - slot + rev_in[...]).astype(F32)

    def turn(c):
        cols[c] = field[c].T

    loop(NBLOCK, turn)

    def rows_of(ref, g):
        return ref[pl.ds(g * N_DST, N_DST)].reshape(CHUNK, WIDTH)

    def put_rows(ref, g, value):
        ref[pl.ds(g * N_DST, N_DST)] = value.reshape(N_DST, CAP, WIDTH)

    def live_of(g):
        return cols[pl.ds(g * BPC, BPC), :, HARM : HARM + 1].reshape(CHUNK, 1)

    def lower(level, g, value):
        low = lax.dot_general(
            value, down[level], (((1,), (1,)), ((), ())), preferred_element_type=F32
        )
        low = (silu(low) * live_of(g)).astype(BF16)
        for i in range(BPC):
            c = g * BPC + i
            modes = dot(rows_y[c], low[i * BLK : (i + 1) * BLK])
            pool[s * NBLOCK + c] = jnp.concatenate(
                [modes[: HPAD // 2], modes[HPAD // 2 :]], axis=1
            ).astype(BF16)

    def share(start, count):
        piece = pool.at[pl.ds(s * NBLOCK + start, count)]
        for hop in range(1, N_SRC):
            remote(
                piece, piece, pool_send, pool_recv.at[s], (s + hop) % N_SRC, d
            ).start()

    def span(g):
        return pl.ds(pl.multiple_of(g * CHUNK, CHUNK), CHUNK)

    def base_of(level, g):
        base[span(g), :] = dot(rows_of(state, g), edge[level, 0])

    loads[0].wait()
    loads[1].wait()
    loop(N_SRC, lambda g: lower(0, g, rows_of(state, g)))
    pl.semaphore_wait(barrier, DEVS - 1)
    share(0, NBLOCK)

    def choose(c):
        column = cols[c]
        source = column[:, HARM + 1 : HARM + 2]
        target = column[:, HARM + 2 : HARM + 3]
        alive = column[:, HARM : HARM + 1]
        pick[c] = (source == iota((BLK, 2 * ATOM_ROWS), 1).astype(F32)).astype(F32).astype(BF16)
        same = (target == iota((BLK, BLK), 1).astype(F32)).astype(F32)
        mirror[c] = (same * alive).astype(BF16)
        onehot[c] = (
            (iota((ATOM_ROWS, BLK), 0) == dst_in[pl.ds(c, 1), :]).astype(F32).astype(BF16)
        )

    loop(NBLOCK, choose)
    loads[2].wait()
    loop(N_SRC, lambda g: base_of(0, g))
    loads[3].wait()
    mode = iota((HPAD, 4 * TRIP), 0)
    degree = (
        (mode >= 3).astype(jnp.int32)
        + (mode >= 8).astype(jnp.int32)
        + (mode >= 15).astype(jnp.int32)
    )
    keep = (degree == iota((HPAD, 4 * TRIP), 1) // TRIP).astype(F32) * (BLK * PAIRS) ** (-0.5)

    def run_level(level):
        drain(pool.at[pl.ds(0, (N_SRC - 1) * NBLOCK)], pool_send)
        for hop in range(1, N_SRC):
            owner = (s + hop) % N_SRC
            drain(pool.at[pl.ds(owner * NBLOCK, NBLOCK)], pool_recv.at[owner])

        def mix(c):
            modes = pool[tri[0, c]].astype(F32)
            for q in range(1, PAIRS):
                modes += pool[tri[q, c]].astype(F32)
            modes = jnp.concatenate([modes[:, :TRIP], modes[:, TRIP:]], axis=0)
            spectrum[c] = (jnp.concatenate([modes] * 4, axis=1) * keep).astype(BF16)

        loop(NBLOCK, mix)
        lifted[...] = (
            dot(spectrum[...].reshape(NBLOCK * HPAD, 4 * TRIP), trip[level])
            .astype(BF16)
            .reshape(NBLOCK, HPAD, WIDTH)
        )

        def talk(j):
            g = (s + 1 + j) % N_SRC
            parts = [
                dot(cols[g * BPC + i].astype(BF16), lifted[g * BPC + i]) for i in range(BPC)
            ]
            pre = base[span(g), :] + jnp.concatenate(parts, axis=0)
            put_rows(msg, g, (silu(pre) * live_of(g)).astype(BF16))

            def send(i):
                t = (d + 1 + i) % N_DST
                b = g * N_DST + t

                @pl.when(b != me)
                def _():
                    remote(msg.at[b], arr.at[me], msg_send, msg_recv.at[s], g, t).start()

            loop(N_DST, send)

        loop(N_SRC, talk)

        def listen(j):
            g = (s + N_SRC - 1 - j) % N_SRC

            @pl.when(g != s)
            def _():
                drain(arr.at[pl.ds(g * N_DST, N_DST)], msg_recv.at[g])

            @pl.when(g == s)
            def _():
                drain(arr.at[pl.ds(0, N_DST - 1)], msg_recv.at[g])

            came = rows_of(arr, g)
            mirrored = jnp.concatenate(
                [
                    dot(mirror[g * BPC + i], came[i * BLK : (i + 1) * BLK])
                    for i in range(BPC)
                ],
                axis=0,
            )
            symmetric = (rows_of(msg, g).astype(F32) + mirrored).astype(BF16)
            inner = silu(dot(symmetric, edge[level, 1])).astype(BF16)
            value = (symmetric.astype(F32) + dot(inner, edge[level, 2])).astype(BF16)
            put_rows(refined, g, value)
            sums = total[...]
            for i in range(BPC):
                sums += dot(onehot[g * BPC + i], value[i * BLK : (i + 1) * BLK])
            total[...] = sums
            base[span(g), :] = dot(value, edge[level, 3])

        loop(N_SRC, listen)
        part[...] = total[...].astype(BF16).reshape(N_SRC, PIECE, WIDTH)
        for hop in range(N_SRC):
            t = (s + hop) % N_SRC
            td = ((z + t // 2) % 4) * 4 + y

            @pl.when((t != s) | (td != d))
            def _():
                remote(
                    part.at[t], gathered.at[s], part_send, part_recv, t, td
                ).start()

        home = ((z + 4 - x) % 4) * 4 + y
        total[...] = jnp.zeros_like(total)
        drain(arr.at[pl.ds(0, DEVS - 1)], msg_send)

        @pl.when(home == d)
        def _():
            gathered[pl.ds(s, 1)] = part[pl.ds(s, 1)]
            drain(gathered.at[pl.ds(0, N_SRC - 1)], part_recv)
            drain(gathered.at[pl.ds(0, N_SRC - 1)], part_send)

        @pl.when(home != d)
        def _():
            drain(gathered, part_recv)
            drain(gathered, part_send)

        sums = gathered[0].astype(F32)
        for i in range(1, N_SRC):
            sums += gathered[i].astype(F32)
        sums = (sums * DEGREE ** (-0.5)).astype(BF16)
        atoms[...] = sums
        near = home // 2
        slot = home % 2

        def spread(i):
            t = (d + 1 + i) % N_DST

            @pl.when(near * N_DST + t != me)
            def _():
                remote(atoms, region.at[slot, s], atom_send, atom_recv, near, t).start()

        loop(N_DST, spread)

        @pl.when(near == s)
        def _():
            region[pl.ds(slot, 1), pl.ds(s, 1)] = sums[None, None]
            drain(arr.at[pl.ds(0, 2 * (N_DST - 1))], atom_recv)
            drain(arr.at[pl.ds(0, 2 * (N_DST - 1))], atom_send)

        @pl.when(near != s)
        def _():
            drain(arr.at[pl.ds(0, 2 * N_DST)], atom_recv)
            drain(arr.at[pl.ds(0, 2 * N_DST)], atom_send)

        known = dot(region[...].reshape(2 * ATOM_ROWS, WIDTH), edge[level, 3]).astype(BF16)
        region[...] = known.reshape(region.shape)

        def update(g):
            chosen = pick[pl.ds(g * BPC, BPC)].reshape(CHUNK, 2 * ATOM_ROWS)
            feed = dot(chosen, region[...].reshape(2 * ATOM_ROWS, WIDTH))
            first = silu(base[span(g), :] + feed).astype(BF16)
            second = silu(dot(first, edge[level, 4])).astype(BF16)
            fresh = (
                rows_of(state, g).astype(F32)
                + rows_of(refined, g).astype(F32)
                + dot(second, edge[level, 5])
            )
            fresh = (fresh * (live_of(g) * 0.5**0.5)).astype(BF16)
            put_rows(state, g, fresh)

            @pl.when(level < NBLK - 1)
            def _():
                lower(level + 1, g, fresh)
                share(g * BPC, BPC)

            @pl.when(level == NBLK - 1)
            def _():
                piece = pl.ds(g * N_DST, N_DST)
                pltpu.make_async_copy(state.at[piece], out.at[piece], out_sem).start()

        loop(N_SRC, update)

        @pl.when(level < NBLK - 1)
        def _():
            loop(N_SRC, lambda g: base_of(level + 1, g))

    loop(NBLK, run_level)
    drain(state, out_sem)


def body(
    edge_state, directions, src_atom, dst_atom, rev_pos, counts, triplets, down_w, trip_w, edge_w
):
    vmem = pl.BlockSpec(memory_space=pltpu.VMEM)
    hbm = pl.BlockSpec(memory_space=pl.ANY)
    dma = pltpu.SemaphoreType.DMA
    down = jnp.swapaxes(down_w, 1, 2)
    edges = pltpu.VMEM((DEVS, CAP, WIDTH), BF16)
    out = pl.pallas_call(
        kernel,
        out_shape=jax.ShapeDtypeStruct((DEVS, CAP, WIDTH), BF16),
        in_specs=[pl.BlockSpec(memory_space=pltpu.SMEM)] + [vmem] * 5 + [hbm] * 4,
        out_specs=hbm,
        scratch_shapes=[
            edges,
            pltpu.VMEM((ROWS, WIDTH), F32),
            edges,
            edges,
            edges,
            pltpu.VMEM((NBLOCK, 8, BLK), F32),
            pltpu.VMEM((NBLOCK, HPAD, BLK), F32),
            pltpu.VMEM((NBLOCK, HPAD, BLK), BF16),
            pltpu.VMEM((NBLOCK, BLK, HPAD), F32),
            pltpu.VMEM((N_SRC * NBLOCK, HPAD // 2, 2 * TRIP), BF16),
            pltpu.VMEM((NBLOCK, HPAD, 4 * TRIP), BF16),
            pltpu.VMEM((NBLOCK, HPAD, WIDTH), BF16),
            pltpu.VMEM((NBLOCK, ATOM_ROWS, BLK), BF16),
            pltpu.VMEM((NBLOCK, BLK, BLK), BF16),
            pltpu.VMEM((NBLOCK, BLK, 2 * ATOM_ROWS), BF16),
            pltpu.VMEM(down.shape, BF16),
            pltpu.VMEM(trip_w.shape, BF16),
            pltpu.VMEM(edge_w.shape, BF16),
            pltpu.VMEM((ATOM_ROWS, WIDTH), F32),
            pltpu.VMEM((N_SRC, PIECE, WIDTH), BF16),
            pltpu.VMEM((N_SRC, PIECE, WIDTH), BF16),
            pltpu.VMEM((PIECE, WIDTH), BF16),
            pltpu.VMEM((2, N_SRC, PIECE, WIDTH), BF16),
            dma((4,)),
            dma,
            dma,
            dma((N_SRC,)),
            dma,
            dma((N_SRC,)),
            dma,
            dma,
            dma,
            dma,
        ],
        compiler_params=pltpu.CompilerParams(
            collective_id=0, has_side_effects=True, vmem_limit_bytes=60 << 20
        ),
    )(
        triplets.T,
        directions,
        src_atom.reshape(NBLOCK, BLK),
        dst_atom.reshape(NBLOCK, BLK),
        rev_pos.reshape(NBLOCK, BLK),
        counts,
        edge_state.reshape(DEVS, CAP, WIDTH),
        down,
        trip_w,
        edge_w,
    )
    return out.reshape(ROWS, WIDTH)


def solution(mesh):
    placed = (
        P(("src", "dst"), None),
        P(None, ("src", "dst")),
        P(("src", "dst")),
        P(("src", "dst")),
        P(("src", "dst")),
        P(("src", "dst"), None),
        P(("src", "dst"), None),
        P(),
        P(),
        P(),
    )
    return jax.shard_map(
        body, mesh=mesh, in_specs=placed, out_specs=P(("src", "dst"), None), check_vma=False
    )
```

```python
import jax
import jax.numpy as jnp
from jax import lax
from jax.experimental import pallas as pl
from jax.experimental.pallas import tpu as pltpu
from jax.sharding import PartitionSpec as P

BLK = 128
PAIRS = 4
NBLK = 2
HARM = 24
HPAD = 32
TRIP = 64
DEGREE = 64
N_SRC = 8
N_DST = 16
DEVS = N_SRC * N_DST
CAP = 16
WIDTH = 512
ROWS = DEVS * CAP
CHUNK = N_DST * CAP
NBLOCK = ROWS // BLK
BPC = CHUNK // BLK
MIX = 4
WIDE = 2
ATOM_ROWS = 256
PIECE = ATOM_ROWS // N_SRC
FAR = sorted(
    ((i, j) for i in range(4) for j in range(4)),
    key=lambda p: -min(p[0], 4 - p[0]) - min(p[1], 4 - p[1]),
)
MESH = pl.DeviceIdType.MESH
F32 = jnp.float32
BF16 = jnp.bfloat16


def silu(value):
    half = 0.5 * value
    return half + half * jnp.tanh(half)


def dot(a, b):
    return jnp.dot(a, b, preferred_element_type=F32)


def loop(count, step):
    def body(i, carry):
        step(i)
        return carry

    lax.fori_loop(0, count, body, 0)


def harmonics(x, y, z):
    xx, yy, zz = x * x, y * y, z * z
    diff = xx - yy
    r3, r5, r15, r35 = 3.0**0.5, 5.0**0.5, 15.0**0.5, 35.0**0.5
    r38, r58, r358 = 0.375**0.5, 0.625**0.5, 4.375**0.5
    return [
        x,
        y,
        z,
        r3 * x * y,
        r3 * y * z,
        r3 * x * z,
        0.5 * r3 * diff,
        1.5 * zz - 0.5,
        r58 * y * (3.0 * xx - yy),
        r15 * x * y * z,
        r38 * y * (5.0 * zz - 1.0),
        0.5 * z * (5.0 * zz - 3.0),
        r38 * x * (5.0 * zz - 1.0),
        0.5 * r15 * z * diff,
        r58 * x * (xx - 3.0 * yy),
        0.5 * r35 * x * y * diff,
        r358 * y * z * (3.0 * xx - yy),
        0.5 * r5 * x * y * (7.0 * zz - 1.0),
        r58 * y * z * (7.0 * zz - 3.0),
        0.125 * (35.0 * zz * zz - 30.0 * zz + 3.0),
        r58 * x * z * (7.0 * zz - 3.0),
        0.25 * r5 * diff * (7.0 * zz - 1.0),
        r358 * x * z * (xx - 3.0 * yy),
        0.125 * r35 * (xx * xx - 6.0 * xx * yy + yy * yy),
    ]


def kernel(
    tri,
    dirs_in,
    src_in,
    dst_in,
    rev_in,
    counts_in,
    state_in,
    down_in,
    trip_in,
    edge_in,
    out,
    state,
    base,
    msg,
    arr,
    refined,
    split,
    field,
    rows_y,
    cols,
    pool,
    spectrum,
    lifted,
    onehot,
    mirror,
    pick,
    down,
    trip,
    edge,
    total,
    part,
    gathered,
    atoms,
    region,
    load_sem,
    out_sem,
    pool_send,
    pool_recv,
    msg_send,
    msg_recv,
    part_send,
    part_recv,
    atom_send,
    atom_recv,
):
    s = lax.axis_index("src")
    d = lax.axis_index("dst")
    me = s * N_DST + d
    x = s // 2
    core = s % 2
    z = d // 4
    y = d % 4

    def remote(src, dst, send, recv, ts, td):
        return pltpu.make_async_remote_copy(
            src_ref=src,
            dst_ref=dst,
            send_sem=send,
            recv_sem=recv,
            device_id=(ts, td),
            device_id_type=MESH,
        )

    def drain(ref, sem):
        pltpu.make_async_copy(ref, ref, sem).wait()

    barrier = pltpu.get_barrier_semaphore()

    loads = [
        pltpu.make_async_copy(a, b, load_sem.at[i])
        for i, (a, b) in enumerate(
            [(state_in, state), (down_in, down), (edge_in, edge), (trip_in, trip)]
        )
    ]
    for load in loads:
        load.start()
    def signal(ts, td):
        pl.semaphore_signal(barrier, inc=1, device_id=(ts, td), device_id_type=MESH)

    lines = [(s + hop) % N_SRC for hop in range(N_SRC)]

    def greet(i):
        td = (d + 1 + i) % N_DST
        for ts in lines:
            signal(ts, td)

    loop(N_DST - 1, greet)
    for ts in lines[1:]:
        signal(ts, d)
    total[...] = jnp.zeros_like(total)
    arr[pl.ds(me, 1)] = jnp.zeros((1, CAP, WIDTH), BF16)

    def iota(shape, axis):
        return lax.broadcasted_iota(jnp.int32, shape, axis)

    lane = iota((NBLOCK, BLK), 1)
    number = iota((NBLOCK, BLK), 0)
    spread_counts = jnp.where(
        lane // (BLK // CAP) == number,
        jnp.broadcast_to(counts_in[...], (NBLOCK, BLK)),
        0,
    ).astype(F32)
    widen = iota((BLK, BLK), 0) % (BLK // CAP) == iota((BLK, BLK), 1) // CAP
    filled = dot(spread_counts.astype(BF16), widen.astype(F32).astype(BF16))
    slot = lane % CAP
    for c in range(NBLOCK):
        split[c, 0:3, :] = dirs_in[:, c * BLK : (c + 1) * BLK]
    field[...] = jnp.zeros_like(field)
    planes = harmonics(split[:, 0, :], split[:, 1, :], split[:, 2, :])
    for i, plane in enumerate(planes):
        field[:, i, :] = plane
    rows_y[...] = field[...].astype(BF16)
    field[:, HARM, :] = (slot.astype(F32) < filled).astype(F32)
    field[:, HARM + 1, :] = src_in[...].astype(F32)
    field[:, HARM + 2, :] = (lane - slot + rev_in[...]).astype(F32)

    def turn(c):
        cols[c] = field[c].T

    loop(NBLOCK, turn)

    def rows_of(ref, g, n=1):
        return ref[pl.ds(g * n * N_DST, n * N_DST)].reshape(n * CHUNK, WIDTH)

    def put_rows(ref, g, value, n=1):
        ref[pl.ds(g * n * N_DST, n * N_DST)] = value.reshape(n * N_DST, CAP, WIDTH)

    def live_of(g, n=1):
        column = cols[pl.ds(g * n * BPC, n * BPC), :, HARM : HARM + 1]
        return column.reshape(n * CHUNK, 1)

    def lower(level, g, value):
        n = value.shape[0] // CHUNK
        low = lax.dot_general(
            value, down[level], (((1,), (1,)), ((), ())), preferred_element_type=F32
        )
        low = (silu(low) * live_of(g, n)).astype(BF16)
        for i in range(n * BPC):
            c = g * n * BPC + i
            modes = dot(rows_y[c], low[i * BLK : (i + 1) * BLK])
            pool[s * NBLOCK + c] = jnp.concatenate(
                [modes[: HPAD // 2], modes[HPAD // 2 :]], axis=1
            ).astype(BF16)

    def share(start, count):
        piece = pool.at[pl.ds(s * NBLOCK + start, count)]
        for hop in range(1, N_SRC):
            remote(
                piece, piece, pool_send, pool_recv.at[s], (s + hop) % N_SRC, d
            ).start()

    def span(g, n=1):
        return pl.ds(pl.multiple_of(g * n * CHUNK, CHUNK), n * CHUNK)

    def base_of(level, g):
        base[span(g), :] = dot(rows_of(state, g), edge[level, 0])

    loads[0].wait()
    loads[1].wait()
    loop(N_SRC, lambda g: lower(0, g, rows_of(state, g)))
    pl.semaphore_wait(barrier, DEVS - 1)
    share(0, NBLOCK)

    def choose(c):
        column = cols[c]
        source = column[:, HARM + 1 : HARM + 2]
        target = column[:, HARM + 2 : HARM + 3]
        alive = column[:, HARM : HARM + 1]
        pick[c] = (source == iota((BLK, 2 * ATOM_ROWS), 1).astype(F32)).astype(F32).astype(BF16)
        same = (target == iota((BLK, BLK), 1).astype(F32)).astype(F32)
        mirror[c] = (same * alive).astype(BF16)
        onehot[c] = (
            (iota((ATOM_ROWS, BLK), 0) == dst_in[pl.ds(c, 1), :]).astype(F32).astype(BF16)
        )

    loop(NBLOCK, choose)
    loads[2].wait()
    loop(N_SRC, lambda g: base_of(0, g))
    loads[3].wait()
    mode = iota((HPAD, 4 * TRIP), 0)
    degree = (
        (mode >= 3).astype(jnp.int32)
        + (mode >= 8).astype(jnp.int32)
        + (mode >= 15).astype(jnp.int32)
    )
    keep = (degree == iota((HPAD, 4 * TRIP), 1) // TRIP).astype(F32) * (BLK * PAIRS) ** (-0.5)

    def run_level(level):
        drain(pool.at[pl.ds(0, (N_SRC - 1) * NBLOCK)], pool_send)
        for hop in range(1, N_SRC):
            owner = (s + hop) % N_SRC
            drain(pool.at[pl.ds(owner * NBLOCK, NBLOCK)], pool_recv.at[owner])

        def mix(i):
            mixed = []
            for k in range(MIX):
                c = i * MIX + k
                modes = [pool[tri[q, c]].astype(F32) for q in range(PAIRS)]
                modes = (modes[0] + modes[1]) + (modes[2] + modes[3])
                modes = jnp.concatenate([modes[:, :TRIP], modes[:, TRIP:]], axis=0)
                mixed.append((jnp.concatenate([modes] * 4, axis=1) * keep).astype(BF16))
            spectrum[pl.ds(i * MIX, MIX)] = jnp.stack(mixed)

        loop(NBLOCK // MIX, mix)
        lifted[...] = (
            dot(spectrum[...].reshape(NBLOCK * HPAD, 4 * TRIP), trip[level])
            .astype(BF16)
            .reshape(NBLOCK, HPAD, WIDTH)
        )

        def talk(j):
            g = (s + 1 + j) % N_SRC
            parts = [
                dot(cols[g * BPC + i].astype(BF16), lifted[g * BPC + i]) for i in range(BPC)
            ]
            pre = base[span(g), :] + jnp.concatenate(parts, axis=0)
            put_rows(msg, g, (silu(pre) * live_of(g)).astype(BF16))

            def send(i):
                for k in range(4):
                    t = (d + 1 + i * 4 + k) % N_DST
                    b = g * N_DST + t

                    @pl.when(b != me)
                    def _():
                        remote(msg.at[b], arr.at[me], msg_send, msg_recv.at[s], g, t).start()

            loop(N_DST // 4, send)

        loop(N_SRC, talk)

        def listen(j):
            g = (s + N_SRC - 1 - j) % N_SRC

            @pl.when(g != s)
            def _():
                drain(arr.at[pl.ds(g * N_DST, N_DST)], msg_recv.at[g])

            @pl.when(g == s)
            def _():
                drain(arr.at[pl.ds(0, N_DST - 1)], msg_recv.at[g])

            came = rows_of(arr, g)
            mirrored = jnp.concatenate(
                [
                    dot(mirror[g * BPC + i], came[i * BLK : (i + 1) * BLK])
                    for i in range(BPC)
                ],
                axis=0,
            )
            symmetric = (rows_of(msg, g).astype(F32) + mirrored).astype(BF16)
            inner = silu(dot(symmetric, edge[level, 1])).astype(BF16)
            value = (symmetric.astype(F32) + dot(inner, edge[level, 2])).astype(BF16)
            put_rows(refined, g, value)
            sums = total[...]
            for i in range(BPC):
                sums += dot(onehot[g * BPC + i], value[i * BLK : (i + 1) * BLK])
            total[...] = sums

        loop(N_SRC, listen)
        part[...] = total[...].astype(BF16).reshape(N_SRC, PIECE, WIDTH)
        for hop in range(N_SRC):
            t = (s + hop) % N_SRC
            td = ((z + t // 2 + 2 * (t % 2)) % 4) * 4 + y

            @pl.when((t != s) | (td != d))
            def _():
                remote(
                    part.at[t], gathered.at[s], part_send, part_recv, t, td
                ).start()

        def ahead(g):
            base[span(g), :] = dot(rows_of(refined, g), edge[level, 3])

        loop(N_SRC, ahead)
        home = ((z + 8 - x - 2 * core) % 4) * 4 + y
        total[...] = jnp.zeros_like(total)
        drain(arr.at[pl.ds(0, DEVS - 1)], msg_send)

        @pl.when(home == d)
        def _():
            gathered[pl.ds(s, 1)] = part[pl.ds(s, 1)]
            drain(gathered.at[pl.ds(0, N_SRC - 1)], part_recv)
            drain(gathered.at[pl.ds(0, N_SRC - 1)], part_send)

        @pl.when(home != d)
        def _():
            drain(gathered, part_recv)
            drain(gathered, part_send)

        sums = gathered[0].astype(F32)
        for i in range(1, N_SRC):
            sums += gathered[i].astype(F32)
        sums = (sums * DEGREE ** (-0.5)).astype(BF16)
        atoms[...] = sums
        near = home // 2
        slot = home % 2

        for far in FAR:
            t = ((z + far[0]) % 4) * 4 + (y + far[1]) % 4

            @pl.when(near * N_DST + t != me)
            def _():
                remote(atoms, region.at[slot, s], atom_send, atom_recv, near, t).start()

        @pl.when(near == s)
        def _():
            region[pl.ds(slot, 1), pl.ds(s, 1)] = sums[None, None]
            drain(arr.at[pl.ds(0, 2 * (N_DST - 1))], atom_recv)
            drain(arr.at[pl.ds(0, 2 * (N_DST - 1))], atom_send)

        @pl.when(near != s)
        def _():
            drain(arr.at[pl.ds(0, 2 * N_DST)], atom_recv)
            drain(arr.at[pl.ds(0, 2 * N_DST)], atom_send)

        known = dot(region[...].reshape(2 * ATOM_ROWS, WIDTH), edge[level, 3]).astype(BF16)
        region[...] = known.reshape(region.shape)

        def update(g):
            chosen = pick[pl.ds(g * WIDE * BPC, WIDE * BPC)]
            chosen = chosen.reshape(WIDE * CHUNK, 2 * ATOM_ROWS)
            feed = dot(chosen, region[...].reshape(2 * ATOM_ROWS, WIDTH))
            first = silu(base[span(g, WIDE), :] + feed).astype(BF16)
            second = silu(dot(first, edge[level, 4])).astype(BF16)
            fresh = (
                rows_of(state, g, WIDE).astype(F32)
                + rows_of(refined, g, WIDE).astype(F32)
                + dot(second, edge[level, 5])
            )
            fresh = (fresh * (live_of(g, WIDE) * 0.5**0.5)).astype(BF16)
            put_rows(state, g, fresh, WIDE)

            @pl.when(level < NBLK - 1)
            def _():
                lower(level + 1, g, fresh)
                share(g * WIDE * BPC, WIDE * BPC)

            @pl.when(level == NBLK - 1)
            def _():
                piece = pl.ds(g * WIDE * N_DST, WIDE * N_DST)
                pltpu.make_async_copy(state.at[piece], out.at[piece], out_sem).start()

        loop(N_SRC // WIDE, update)

        @pl.when(level < NBLK - 1)
        def _():
            loop(N_SRC, lambda g: base_of(level + 1, g))

    loop(NBLK, run_level)
    drain(state, out_sem)


def body(
    edge_state, directions, src_atom, dst_atom, rev_pos, counts, triplets, down_w, trip_w, edge_w
):
    vmem = pl.BlockSpec(memory_space=pltpu.VMEM)
    hbm = pl.BlockSpec(memory_space=pl.ANY)
    dma = pltpu.SemaphoreType.DMA
    down = jnp.swapaxes(down_w, 1, 2)
    edges = pltpu.VMEM((DEVS, CAP, WIDTH), BF16)
    out = pl.pallas_call(
        kernel,
        out_shape=jax.ShapeDtypeStruct((DEVS, CAP, WIDTH), BF16),
        in_specs=[pl.BlockSpec(memory_space=pltpu.SMEM)] + [vmem] * 5 + [hbm] * 4,
        out_specs=hbm,
        scratch_shapes=[
            edges,
            pltpu.VMEM((ROWS, WIDTH), F32),
            edges,
            edges,
            edges,
            pltpu.VMEM((NBLOCK, 8, BLK), F32),
            pltpu.VMEM((NBLOCK, HPAD, BLK), F32),
            pltpu.VMEM((NBLOCK, HPAD, BLK), BF16),
            pltpu.VMEM((NBLOCK, BLK, HPAD), F32),
            pltpu.VMEM((N_SRC * NBLOCK, HPAD // 2, 2 * TRIP), BF16),
            pltpu.VMEM((NBLOCK, HPAD, 4 * TRIP), BF16),
            pltpu.VMEM((NBLOCK, HPAD, WIDTH), BF16),
            pltpu.VMEM((NBLOCK, ATOM_ROWS, BLK), BF16),
            pltpu.VMEM((NBLOCK, BLK, BLK), BF16),
            pltpu.VMEM((NBLOCK, BLK, 2 * ATOM_ROWS), BF16),
            pltpu.VMEM(down.shape, BF16),
            pltpu.VMEM(trip_w.shape, BF16),
            pltpu.VMEM(edge_w.shape, BF16),
            pltpu.VMEM((ATOM_ROWS, WIDTH), F32),
            pltpu.VMEM((N_SRC, PIECE, WIDTH), BF16),
            pltpu.VMEM((N_SRC, PIECE, WIDTH), BF16),
            pltpu.VMEM((PIECE, WIDTH), BF16),
            pltpu.VMEM((2, N_SRC, PIECE, WIDTH), BF16),
            dma((4,)),
            dma,
            dma,
            dma((N_SRC,)),
            dma,
            dma((N_SRC,)),
            dma,
            dma,
            dma,
            dma,
        ],
        compiler_params=pltpu.CompilerParams(
            collective_id=0, has_side_effects=True, vmem_limit_bytes=60 << 20
        ),
    )(
        triplets.T,
        directions,
        src_atom.reshape(NBLOCK, BLK),
        dst_atom.reshape(NBLOCK, BLK),
        rev_pos.reshape(NBLOCK, BLK),
        counts,
        edge_state.reshape(DEVS, CAP, WIDTH),
        down,
        trip_w,
        edge_w,
    )
    return out.reshape(ROWS, WIDTH)


def solution(mesh):
    placed = (
        P(("src", "dst"), None),
        P(None, ("src", "dst")),
        P(("src", "dst")),
        P(("src", "dst")),
        P(("src", "dst")),
        P(("src", "dst"), None),
        P(("src", "dst"), None),
        P(),
        P(),
        P(),
    )
    return jax.shard_map(
        body, mesh=mesh, in_specs=placed, out_specs=P(("src", "dst"), None), check_vma=False
    )
```

```python
import jax
import jax.numpy as jnp
from jax import lax
from jax.experimental import pallas as pl
from jax.experimental.pallas import tpu as pltpu
from jax.sharding import PartitionSpec as P

BLK = 128
PAIRS = 4
NBLK = 2
HARM = 24
HPAD = 32
TRIP = 64
DEGREE = 64
N_SRC = 8
N_DST = 16
DEVS = N_SRC * N_DST
CAP = 16
WIDTH = 512
ROWS = DEVS * CAP
CHUNK = N_DST * CAP
NBLOCK = ROWS // BLK
BPC = CHUNK // BLK
MIX = 4
WIDE = 2
ATOM_ROWS = 256
PIECE = ATOM_ROWS // N_SRC
FAR = sorted(
    ((i, j) for i in range(4) for j in range(4)),
    key=lambda p: -min(p[0], 4 - p[0]) - min(p[1], 4 - p[1]),
)
MESH = pl.DeviceIdType.MESH
F32 = jnp.float32
BF16 = jnp.bfloat16


def silu_of_half(half):
    return half + half * jnp.tanh(half)


def dot(a, b):
    return jnp.dot(a, b, preferred_element_type=F32)


def loop(count, step):
    def body(i, carry):
        step(i)
        return carry

    lax.fori_loop(0, count, body, 0)


def harmonics(x, y, z):
    xx, yy, zz = x * x, y * y, z * z
    diff = xx - yy
    r3, r5, r15, r35 = 3.0**0.5, 5.0**0.5, 15.0**0.5, 35.0**0.5
    r38, r58, r358 = 0.375**0.5, 0.625**0.5, 4.375**0.5
    return [
        x,
        y,
        z,
        r3 * x * y,
        r3 * y * z,
        r3 * x * z,
        0.5 * r3 * diff,
        1.5 * zz - 0.5,
        r58 * y * (3.0 * xx - yy),
        r15 * x * y * z,
        r38 * y * (5.0 * zz - 1.0),
        0.5 * z * (5.0 * zz - 3.0),
        r38 * x * (5.0 * zz - 1.0),
        0.5 * r15 * z * diff,
        r58 * x * (xx - 3.0 * yy),
        0.5 * r35 * x * y * diff,
        r358 * y * z * (3.0 * xx - yy),
        0.5 * r5 * x * y * (7.0 * zz - 1.0),
        r58 * y * z * (7.0 * zz - 3.0),
        0.125 * (35.0 * zz * zz - 30.0 * zz + 3.0),
        r58 * x * z * (7.0 * zz - 3.0),
        0.25 * r5 * diff * (7.0 * zz - 1.0),
        r358 * x * z * (xx - 3.0 * yy),
        0.125 * r35 * (xx * xx - 6.0 * xx * yy + yy * yy),
    ]


def kernel(
    tri,
    dirs_in,
    src_in,
    dst_in,
    rev_in,
    counts_in,
    state_in,
    down_in,
    trip_in,
    edge_in,
    state,
    base,
    msg,
    arr,
    refined,
    split,
    field,
    rows_y,
    cols,
    pool,
    spectrum,
    lifted,
    onehot,
    mirror,
    pick,
    down,
    trip,
    edge,
    total,
    part,
    gathered,
    atoms,
    region,
    load_sem,
    pool_send,
    pool_recv,
    msg_send,
    msg_recv,
    part_send,
    part_recv,
    atom_send,
    atom_recv,
):
    s = lax.axis_index("src")
    d = lax.axis_index("dst")
    me = s * N_DST + d
    x = s // 2
    core = s % 2
    z = d // 4
    y = d % 4

    def remote(src, dst, send, recv, ts, td):
        return pltpu.make_async_remote_copy(
            src_ref=src,
            dst_ref=dst,
            send_sem=send,
            recv_sem=recv,
            device_id=(ts, td),
            device_id_type=MESH,
        )

    def drain(ref, sem):
        pltpu.make_async_copy(ref, ref, sem).wait()

    barrier = pltpu.get_barrier_semaphore()

    loads = [
        pltpu.make_async_copy(a, b, load_sem.at[i])
        for i, (a, b) in enumerate(
            [(state_in, state), (down_in, down), (edge_in, edge), (trip_in, trip)]
        )
    ]
    for load in loads:
        load.start()
    def signal(ts, td):
        pl.semaphore_signal(barrier, inc=1, device_id=(ts, td), device_id_type=MESH)

    lines = [(s + hop) % N_SRC for hop in range(N_SRC)]

    def greet(i):
        td = (d + 1 + i) % N_DST
        for ts in lines:
            signal(ts, td)

    loop(N_DST - 1, greet)
    for ts in lines[1:]:
        signal(ts, d)
    total[...] = jnp.zeros_like(total)
    arr[pl.ds(me, 1)] = jnp.zeros((1, CAP, WIDTH), BF16)

    def iota(shape, axis):
        return lax.broadcasted_iota(jnp.int32, shape, axis)

    lane = iota((NBLOCK, BLK), 1)
    number = iota((NBLOCK, BLK), 0)
    spread_counts = jnp.where(
        lane // (BLK // CAP) == number,
        jnp.broadcast_to(counts_in[...], (NBLOCK, BLK)),
        0,
    ).astype(F32)
    widen = iota((BLK, BLK), 0) % (BLK // CAP) == iota((BLK, BLK), 1) // CAP
    filled = dot(spread_counts.astype(BF16), widen.astype(F32).astype(BF16))
    slot = lane % CAP
    for c in range(NBLOCK):
        split[c, 0:3, :] = dirs_in[:, c * BLK : (c + 1) * BLK]
    field[...] = jnp.zeros_like(field)
    planes = harmonics(split[:, 0, :], split[:, 1, :], split[:, 2, :])
    for i, plane in enumerate(planes):
        field[:, i, :] = plane
    rows_y[...] = field[...].astype(BF16)
    field[:, HARM, :] = (slot.astype(F32) < filled).astype(F32)
    field[:, HARM + 1, :] = src_in[...].astype(F32)
    field[:, HARM + 2, :] = (lane - slot + rev_in[...]).astype(F32)

    def turn(c):
        cols[c] = field[c].T

    loop(NBLOCK, turn)

    def rows_of(ref, g, n=1):
        return ref[pl.ds(g * n * N_DST, n * N_DST)].reshape(n * CHUNK, WIDTH)

    def put_rows(ref, g, value, n=1):
        ref[pl.ds(g * n * N_DST, n * N_DST)] = value.reshape(n * N_DST, CAP, WIDTH)

    def live_of(g, n=1):
        column = cols[pl.ds(g * n * BPC, n * BPC), :, HARM : HARM + 1]
        return column.reshape(n * CHUNK, 1)

    def lower(level, g, value):
        n = value.shape[0] // CHUNK
        low = lax.dot_general(
            value, down[level], (((1,), (1,)), ((), ())), preferred_element_type=F32
        )
        low = (silu_of_half(low) * live_of(g, n)).astype(BF16)
        modes = []
        for i in range(n * BPC):
            c = g * n * BPC + i
            modes.append(dot(rows_y[c], low[i * BLK : (i + 1) * BLK])[:HARM])
        for i in range(n):
            pool[s * N_SRC + g * n + i] = jnp.concatenate(
                [modes[2 * i], modes[2 * i + 1]], axis=1
            ).astype(BF16)

    def share(start, count):
        piece = pool.at[pl.ds(s * N_SRC + start, count)]
        for hop in range(1, N_SRC):
            remote(
                piece, piece, pool_send, pool_recv.at[s], (s + hop) % N_SRC, d
            ).start()

    def span(g, n=1):
        return pl.ds(pl.multiple_of(g * n * CHUNK, CHUNK), n * CHUNK)

    def base_of(level, g):
        base[span(g), :] = dot(rows_of(state, g), edge[level, 0])

    loads[0].wait()
    loads[1].wait()
    down[...] = down[...] * 0.5
    loop(N_SRC, lambda g: lower(0, g, rows_of(state, g)))
    pl.semaphore_wait(barrier, DEVS - 1)
    share(0, N_SRC)

    def choose(c):
        column = cols[c]
        source = column[:, HARM + 1 : HARM + 2]
        target = column[:, HARM + 2 : HARM + 3]
        alive = column[:, HARM : HARM + 1]
        pick[c] = (source == iota((BLK, 2 * ATOM_ROWS), 1).astype(F32)).astype(F32).astype(BF16)
        same = (target == iota((BLK, BLK), 1).astype(F32)).astype(F32)
        mirror[c] = (same * alive).astype(BF16)
        onehot[c] = (
            (iota((ATOM_ROWS, BLK), 0) == dst_in[pl.ds(c, 1), :]).astype(F32).astype(BF16)
        )

    loop(NBLOCK, choose)

    def halve(level):
        for i in (0, 1, 3, 4):
            edge[level, i] = edge[level, i] * 0.5

    loads[2].wait()
    loop(NBLK, halve)
    loop(N_SRC, lambda g: base_of(0, g))
    loads[3].wait()
    mode = iota((HARM, 4 * TRIP), 0)
    degree = (
        (mode >= 3).astype(jnp.int32)
        + (mode >= 8).astype(jnp.int32)
        + (mode >= 15).astype(jnp.int32)
    )
    keep = (degree == iota((HARM, 4 * TRIP), 1) // TRIP).astype(F32) * (0.5 * (BLK * PAIRS) ** (-0.5))

    side = iota((HARM, 2 * TRIP), 1) // TRIP

    def run_level(level):
        drain(pool.at[pl.ds(0, (N_SRC - 1) * N_SRC)], pool_send)
        for hop in range(1, N_SRC):
            owner = (s + hop) % N_SRC
            drain(pool.at[pl.ds(owner * N_SRC, N_SRC)], pool_recv.at[owner])

        def mix(i):
            mixed = []
            for k in range(MIX):
                c = i * MIX + k
                modes = []
                for q in range(PAIRS):
                    block = pool[lax.div(tri[q, c], 2)].astype(F32)
                    wanted = side == lax.rem(tri[q, c], 2)
                    modes.append(jnp.where(wanted, block, 0.0))
                modes = (modes[0] + modes[1]) + (modes[2] + modes[3])
                modes = modes + pltpu.roll(modes, TRIP, 1)
                modes = jnp.concatenate([modes, modes], axis=1) * keep
                modes = jnp.concatenate([modes, jnp.zeros((HPAD - HARM, 4 * TRIP), F32)], axis=0)
                mixed.append(modes.astype(BF16))
            spectrum[pl.ds(i * MIX, MIX)] = jnp.stack(mixed)

        loop(NBLOCK // MIX, mix)
        lifted[...] = (
            dot(spectrum[...].reshape(NBLOCK * HPAD, 4 * TRIP), trip[level])
            .astype(BF16)
            .reshape(NBLOCK, HPAD, WIDTH)
        )

        def talk(j):
            g = (s + 3 + 3 * j) % N_SRC
            parts = [
                dot(cols[g * BPC + i].astype(BF16), lifted[g * BPC + i]) for i in range(BPC)
            ]
            pre = base[span(g), :] + jnp.concatenate(parts, axis=0)
            put_rows(msg, g, (silu_of_half(pre) * live_of(g)).astype(BF16))

            def send(i):
                for k in range(4):
                    t = lax.rem(d + 1 + i * 4 + k, N_DST)
                    b = g * N_DST + t

                    @pl.when(b != me)
                    def _():
                        remote(msg.at[b], arr.at[me], msg_send, msg_recv.at[s], g, t).start()

            loop(N_DST // 4, send)

        loop(N_SRC, talk)

        def listen(j):
            g = (s + 4 * N_SRC - 3 - 3 * j) % N_SRC

            @pl.when(g != s)
            def _():
                drain(arr.at[pl.ds(g * N_DST, N_DST)], msg_recv.at[g])

            @pl.when(g == s)
            def _():
                drain(arr.at[pl.ds(0, N_DST - 1)], msg_recv.at[g])

            came = rows_of(arr, g)
            mirrored = jnp.concatenate(
                [
                    dot(mirror[g * BPC + i], came[i * BLK : (i + 1) * BLK])
                    for i in range(BPC)
                ],
                axis=0,
            )
            symmetric = (rows_of(msg, g).astype(F32) + mirrored).astype(BF16)
            inner = silu_of_half(dot(symmetric, edge[level, 1])).astype(BF16)
            value = (symmetric.astype(F32) + dot(inner, edge[level, 2])).astype(BF16)
            put_rows(refined, g, value)
            sums = total[...]
            for i in range(BPC):
                sums += dot(onehot[g * BPC + i], value[i * BLK : (i + 1) * BLK])
            total[...] = sums

        loop(N_SRC, listen)
        part[...] = total[...].astype(BF16).reshape(N_SRC, PIECE, WIDTH)
        for hop in range(N_SRC):
            t = (s + hop) % N_SRC
            td = ((z + t // 2 + 2 * (t % 2)) % 4) * 4 + y

            @pl.when((t != s) | (td != d))
            def _():
                remote(
                    part.at[t], gathered.at[s], part_send, part_recv, t, td
                ).start()

        def ahead(g):
            base[span(g), :] = dot(rows_of(refined, g), edge[level, 3])

        loop(N_SRC, ahead)
        home = ((z + 8 - x - 2 * core) % 4) * 4 + y
        total[...] = jnp.zeros_like(total)
        drain(arr.at[pl.ds(0, DEVS - 1)], msg_send)

        @pl.when(home == d)
        def _():
            gathered[pl.ds(s, 1)] = part[pl.ds(s, 1)]
            drain(gathered.at[pl.ds(0, N_SRC - 1)], part_recv)
            drain(gathered.at[pl.ds(0, N_SRC - 1)], part_send)

        @pl.when(home != d)
        def _():
            drain(gathered, part_recv)
            drain(gathered, part_send)

        sums = gathered[0].astype(F32)
        for i in range(1, N_SRC):
            sums += gathered[i].astype(F32)
        sums = (sums * DEGREE ** (-0.5)).astype(BF16)
        sums = dot(sums, edge[level, 3]).astype(BF16)
        atoms[...] = sums
        near = home // 2
        slot = home % 2

        for far in FAR:
            t = ((z + far[0]) % 4) * 4 + (y + far[1]) % 4

            @pl.when(near * N_DST + t != me)
            def _():
                remote(atoms, region.at[slot, s], atom_send, atom_recv, near, t).start()

        @pl.when(near == s)
        def _():
            region[pl.ds(slot, 1), pl.ds(s, 1)] = sums[None, None]
            drain(arr.at[pl.ds(0, 2 * (N_DST - 1))], atom_recv)
            drain(arr.at[pl.ds(0, 2 * (N_DST - 1))], atom_send)

        @pl.when(near != s)
        def _():
            drain(arr.at[pl.ds(0, 2 * N_DST)], atom_recv)
            drain(arr.at[pl.ds(0, 2 * N_DST)], atom_send)

        def update(g):
            chosen = pick[pl.ds(g * WIDE * BPC, WIDE * BPC)]
            chosen = chosen.reshape(WIDE * CHUNK, 2 * ATOM_ROWS)
            feed = dot(chosen, region[...].reshape(2 * ATOM_ROWS, WIDTH))
            first = silu_of_half(base[span(g, WIDE), :] + feed).astype(BF16)
            second = silu_of_half(dot(first, edge[level, 4])).astype(BF16)
            fresh = (
                rows_of(state, g, WIDE).astype(F32)
                + rows_of(refined, g, WIDE).astype(F32)
                + dot(second, edge[level, 5])
            )
            fresh = (fresh * (live_of(g, WIDE) * 0.5**0.5)).astype(BF16)
            put_rows(state, g, fresh, WIDE)

            @pl.when(level < NBLK - 1)
            def _():
                lower(level + 1, g, fresh)
                share(g * WIDE, WIDE)

        loop(N_SRC // WIDE, update)

        @pl.when(level < NBLK - 1)
        def _():
            loop(N_SRC, lambda g: base_of(level + 1, g))

    loop(NBLK, run_level)


def body(
    edge_state, directions, src_atom, dst_atom, rev_pos, counts, triplets, down_w, trip_w, edge_w
):
    vmem = pl.BlockSpec(memory_space=pltpu.VMEM)
    hbm = pl.BlockSpec(memory_space=pl.ANY)
    dma = pltpu.SemaphoreType.DMA
    down = jnp.swapaxes(down_w, 1, 2)
    edges = pltpu.VMEM((DEVS, CAP, WIDTH), BF16)
    out = pl.pallas_call(
        kernel,
        out_shape=pltpu.VMEM((DEVS, CAP, WIDTH), BF16),
        in_specs=[pl.BlockSpec(memory_space=pltpu.SMEM)] + [vmem] * 5 + [hbm] * 4,
        out_specs=vmem,
        scratch_shapes=[
            pltpu.VMEM((ROWS, WIDTH), F32),
            edges,
            edges,
            edges,
            pltpu.VMEM((NBLOCK, 8, BLK), F32),
            pltpu.VMEM((NBLOCK, HPAD, BLK), F32),
            pltpu.VMEM((NBLOCK, HPAD, BLK), BF16),
            pltpu.VMEM((NBLOCK, BLK, HPAD), F32),
            pltpu.VMEM((N_SRC * N_SRC, HARM, 2 * TRIP), BF16),
            pltpu.VMEM((NBLOCK, HPAD, 4 * TRIP), BF16),
            pltpu.VMEM((NBLOCK, HPAD, WIDTH), BF16),
            pltpu.VMEM((NBLOCK, ATOM_ROWS, BLK), BF16),
            pltpu.VMEM((NBLOCK, BLK, BLK), BF16),
            pltpu.VMEM((NBLOCK, BLK, 2 * ATOM_ROWS), BF16),
            pltpu.VMEM(down.shape, BF16),
            pltpu.VMEM(trip_w.shape, BF16),
            pltpu.VMEM(edge_w.shape, BF16),
            pltpu.VMEM((ATOM_ROWS, WIDTH), F32),
            pltpu.VMEM((N_SRC, PIECE, WIDTH), BF16),
            pltpu.VMEM((N_SRC, PIECE, WIDTH), BF16),
            pltpu.VMEM((PIECE, WIDTH), BF16),
            pltpu.VMEM((2, N_SRC, PIECE, WIDTH), BF16),
            dma((4,)),
            dma,
            dma((N_SRC,)),
            dma,
            dma((N_SRC,)),
            dma,
            dma,
            dma,
            dma,
        ],
        compiler_params=pltpu.CompilerParams(
            collective_id=0, has_side_effects=True, vmem_limit_bytes=60 << 20
        ),
    )(
        triplets.T,
        directions,
        src_atom.reshape(NBLOCK, BLK),
        dst_atom.reshape(NBLOCK, BLK),
        rev_pos.reshape(NBLOCK, BLK),
        counts,
        edge_state.reshape(DEVS, CAP, WIDTH),
        down,
        trip_w,
        edge_w,
    )
    return out.reshape(ROWS, WIDTH)


def solution(mesh):
    placed = (
        P(("src", "dst"), None),
        P(None, ("src", "dst")),
        P(("src", "dst")),
        P(("src", "dst")),
        P(("src", "dst")),
        P(("src", "dst"), None),
        P(("src", "dst"), None),
        P(),
        P(),
        P(),
    )
    return jax.shard_map(
        body, mesh=mesh, in_specs=placed, out_specs=P(("src", "dst"), None), check_vma=False
    )
```

```python
import jax
import jax.numpy as jnp
from jax import lax
from jax.experimental import pallas as pl
from jax.experimental.pallas import tpu as pltpu
from jax.sharding import PartitionSpec as P

BLK = 128
PAIRS = 4
NBLK = 2
HARM = 24
HPAD = 32
TRIP = 64
DEGREE = 64
N_SRC = 8
N_DST = 16
DEVS = N_SRC * N_DST
CAP = 16
WIDTH = 512
ROWS = DEVS * CAP
CHUNK = N_DST * CAP
NBLOCK = ROWS // BLK
BPC = CHUNK // BLK
MIX = 4
WIDE = 4
ATOM_ROWS = 256
HALVES = 2
PIECE = ATOM_ROWS // N_SRC // HALVES
FAR = sorted(
    ((i, j) for i in range(4) for j in range(4)),
    key=lambda p: -min(p[0], 4 - p[0]) - min(p[1], 4 - p[1]),
)
MESH = pl.DeviceIdType.MESH
F32 = jnp.float32
BF16 = jnp.bfloat16


def silu_of_half(half):
    return half + half * jnp.tanh(half)


def dot(a, b):
    return jnp.dot(a, b, preferred_element_type=F32)


def loop(count, step):
    def body(i, carry):
        step(i)
        return carry

    lax.fori_loop(0, count, body, 0)


def harmonics(x, y, z):
    xx, yy, zz = x * x, y * y, z * z
    diff = xx - yy
    r3, r5, r15, r35 = 3.0**0.5, 5.0**0.5, 15.0**0.5, 35.0**0.5
    r38, r58, r358 = 0.375**0.5, 0.625**0.5, 4.375**0.5
    return [
        x,
        y,
        z,
        r3 * x * y,
        r3 * y * z,
        r3 * x * z,
        0.5 * r3 * diff,
        1.5 * zz - 0.5,
        r58 * y * (3.0 * xx - yy),
        r15 * x * y * z,
        r38 * y * (5.0 * zz - 1.0),
        0.5 * z * (5.0 * zz - 3.0),
        r38 * x * (5.0 * zz - 1.0),
        0.5 * r15 * z * diff,
        r58 * x * (xx - 3.0 * yy),
        0.5 * r35 * x * y * diff,
        r358 * y * z * (3.0 * xx - yy),
        0.5 * r5 * x * y * (7.0 * zz - 1.0),
        r58 * y * z * (7.0 * zz - 3.0),
        0.125 * (35.0 * zz * zz - 30.0 * zz + 3.0),
        r58 * x * z * (7.0 * zz - 3.0),
        0.25 * r5 * diff * (7.0 * zz - 1.0),
        r358 * x * z * (xx - 3.0 * yy),
        0.125 * r35 * (xx * xx - 6.0 * xx * yy + yy * yy),
    ]


def kernel(
    tri,
    dirs_in,
    src_in,
    dst_in,
    rev_in,
    counts_in,
    state_in,
    down_in,
    trip_in,
    edge_in,
    state,
    base,
    msg,
    arr,
    refined,
    split,
    field,
    rows_y,
    cols,
    pool,
    spectrum,
    lifted,
    onehot,
    mirror,
    pick,
    down,
    trip,
    edge,
    total,
    part,
    gathered,
    atoms,
    region,
    load_sem,
    pool_send,
    pool_recv,
    msg_send,
    msg_recv,
    part_send,
    part_recv,
    atom_send,
    atom_recv,
):
    s = lax.axis_index("src")
    d = lax.axis_index("dst")
    me = s * N_DST + d
    x = s // 2
    core = s % 2
    z = d // 4
    y = d % 4

    def remote(src, dst, send, recv, ts, td):
        return pltpu.make_async_remote_copy(
            src_ref=src,
            dst_ref=dst,
            send_sem=send,
            recv_sem=recv,
            device_id=(ts, td),
            device_id_type=MESH,
        )

    def drain(ref, sem):
        pltpu.make_async_copy(ref, ref, sem).wait()

    barrier = pltpu.get_barrier_semaphore()

    loads = [
        pltpu.make_async_copy(a, b, load_sem.at[i])
        for i, (a, b) in enumerate(
            [(state_in, state), (down_in, down), (edge_in, edge), (trip_in, trip)]
        )
    ]
    for load in loads:
        load.start()
    def signal(ts, td):
        pl.semaphore_signal(barrier, inc=1, device_id=(ts, td), device_id_type=MESH)

    lines = [(s + hop) % N_SRC for hop in range(N_SRC)]

    def greet(i):
        td = (d + 1 + i) % N_DST
        for ts in lines:
            signal(ts, td)

    loop(N_DST - 1, greet)
    for ts in lines[1:]:
        signal(ts, d)
    total[...] = jnp.zeros_like(total)
    arr[pl.ds(me, 1)] = jnp.zeros((1, CAP, WIDTH), BF16)

    def iota(shape, axis):
        return lax.broadcasted_iota(jnp.int32, shape, axis)

    lane = iota((NBLOCK, BLK), 1)
    number = iota((NBLOCK, BLK), 0)
    spread_counts = jnp.where(
        lane // (BLK // CAP) == number,
        jnp.broadcast_to(counts_in[...], (NBLOCK, BLK)),
        0,
    ).astype(F32)
    widen = iota((BLK, BLK), 0) % (BLK // CAP) == iota((BLK, BLK), 1) // CAP
    filled = dot(spread_counts.astype(BF16), widen.astype(F32).astype(BF16))
    slot = lane % CAP
    for c in range(NBLOCK):
        split[c, 0:3, :] = dirs_in[:, c * BLK : (c + 1) * BLK]
    field[...] = jnp.zeros_like(field)
    planes = harmonics(split[:, 0, :], split[:, 1, :], split[:, 2, :])
    for i, plane in enumerate(planes):
        field[:, i, :] = plane
    rows_y[...] = field[...].astype(BF16)
    field[:, HARM, :] = (slot.astype(F32) < filled).astype(F32)
    field[:, HARM + 1, :] = src_in[...].astype(F32)
    field[:, HARM + 2, :] = (lane - slot + rev_in[...]).astype(F32)

    def turn(c):
        cols[c] = field[c].T

    loop(NBLOCK, turn)

    def rows_of(ref, g, n=1):
        return ref[pl.ds(g * n * N_DST, n * N_DST)].reshape(n * CHUNK, WIDTH)

    def put_rows(ref, g, value, n=1):
        ref[pl.ds(g * n * N_DST, n * N_DST)] = value.reshape(n * N_DST, CAP, WIDTH)

    def live_of(g, n=1):
        column = cols[pl.ds(g * n * BPC, n * BPC), :, HARM : HARM + 1]
        return column.reshape(n * CHUNK, 1)

    def lower(level, g, value):
        n = value.shape[0] // CHUNK
        low = lax.dot_general(
            value, down[level], (((1,), (1,)), ((), ())), preferred_element_type=F32
        )
        low = (silu_of_half(low) * live_of(g, n)).astype(BF16)
        modes = []
        for i in range(n * BPC):
            c = g * n * BPC + i
            modes.append(dot(rows_y[c], low[i * BLK : (i + 1) * BLK])[:HARM])
        for i in range(n):
            pool[s * N_SRC + g * n + i] = jnp.concatenate(
                [modes[2 * i], modes[2 * i + 1]], axis=1
            ).astype(BF16)

    def share(start, count):
        piece = pool.at[pl.ds(s * N_SRC + start, count)]
        for hop in range(1, N_SRC):
            remote(
                piece, piece, pool_send, pool_recv.at[s], (s + hop) % N_SRC, d
            ).start()

    def span(g, n=1):
        return pl.ds(pl.multiple_of(g * n * CHUNK, CHUNK), n * CHUNK)

    def base_of(level, g):
        base[span(g), :] = dot(rows_of(state, g), edge[level, 0])

    loads[0].wait()
    loads[1].wait()
    down[...] = down[...] * 0.5
    loop(N_SRC // WIDE, lambda g: lower(0, g, rows_of(state, g, WIDE)))
    pl.semaphore_wait(barrier, DEVS - 1)
    share(0, N_SRC)

    def choose(c):
        column = cols[c]
        source = column[:, HARM + 1 : HARM + 2]
        target = column[:, HARM + 2 : HARM + 3]
        alive = column[:, HARM : HARM + 1]
        pick[c] = (source == iota((BLK, 2 * ATOM_ROWS), 1).astype(F32)).astype(F32).astype(BF16)
        same = (target == iota((BLK, BLK), 1).astype(F32)).astype(F32)
        mirror[c] = (same * alive).astype(BF16)
        onehot[c] = (
            (iota((ATOM_ROWS, BLK), 0) == dst_in[pl.ds(c, 1), :]).astype(F32).astype(BF16)
        )

    loop(NBLOCK, choose)

    def halve(level):
        for i in (0, 1, 3, 4):
            edge[level, i] = edge[level, i] * 0.5

    loads[2].wait()
    loop(NBLK, halve)
    loop(N_SRC, lambda g: base_of(0, g))
    loads[3].wait()
    mode = iota((HARM, 4 * TRIP), 0)
    degree = (
        (mode >= 3).astype(jnp.int32)
        + (mode >= 8).astype(jnp.int32)
        + (mode >= 15).astype(jnp.int32)
    )
    keep = (degree == iota((HARM, 4 * TRIP), 1) // TRIP).astype(F32) * (0.5 * (BLK * PAIRS) ** (-0.5))

    side = iota((HARM, 2 * TRIP), 1) // TRIP

    def run_level(level):
        drain(pool.at[pl.ds(0, (N_SRC - 1) * N_SRC)], pool_send)
        for hop in range(1, N_SRC):
            owner = (s + hop) % N_SRC
            drain(pool.at[pl.ds(owner * N_SRC, N_SRC)], pool_recv.at[owner])

        def mix(i):
            mixed = []
            for k in range(MIX):
                c = i * MIX + k
                modes = []
                for q in range(PAIRS):
                    block = pool[lax.div(tri[q, c], 2)].astype(F32)
                    wanted = side == lax.rem(tri[q, c], 2)
                    modes.append(jnp.where(wanted, block, 0.0))
                modes = (modes[0] + modes[1]) + (modes[2] + modes[3])
                modes = modes + pltpu.roll(modes, TRIP, 1)
                modes = jnp.concatenate([modes, modes], axis=1) * keep
                modes = jnp.concatenate([modes, jnp.zeros((HPAD - HARM, 4 * TRIP), F32)], axis=0)
                mixed.append(modes.astype(BF16))
            spectrum[pl.ds(i * MIX, MIX)] = jnp.stack(mixed)

        loop(NBLOCK // MIX, mix)
        lifted[...] = (
            dot(spectrum[...].reshape(NBLOCK * HPAD, 4 * TRIP), trip[level])
            .astype(BF16)
            .reshape(NBLOCK, HPAD, WIDTH)
        )

        def talk(j):
            g = (s + 3 + 3 * j) % N_SRC
            parts = [
                dot(cols[g * BPC + i].astype(BF16), lifted[g * BPC + i]) for i in range(BPC)
            ]
            pre = base[span(g), :] + jnp.concatenate(parts, axis=0)
            put_rows(msg, g, (silu_of_half(pre) * live_of(g)).astype(BF16))

            def send(i):
                for k in range(4):
                    t = lax.rem(z + k + 2, 4) * 4 + lax.rem(y + i + 2, 4)
                    b = g * N_DST + t

                    @pl.when(b != me)
                    def _():
                        remote(msg.at[b], arr.at[me], msg_send, msg_recv.at[s], g, t).start()

            loop(N_DST // 4, send)

        loop(N_SRC, talk)

        def listen(j):
            g = (s + 4 * N_SRC - 3 - 3 * j) % N_SRC

            @pl.when(g != s)
            def _():
                drain(arr.at[pl.ds(g * N_DST, N_DST)], msg_recv.at[g])

            @pl.when(g == s)
            def _():
                drain(arr.at[pl.ds(0, N_DST - 1)], msg_recv.at[g])

            came = rows_of(arr, g)
            mirrored = jnp.concatenate(
                [
                    dot(mirror[g * BPC + i], came[i * BLK : (i + 1) * BLK])
                    for i in range(BPC)
                ],
                axis=0,
            )
            symmetric = (rows_of(msg, g).astype(F32) + mirrored).astype(BF16)
            inner = silu_of_half(dot(symmetric, edge[level, 1])).astype(BF16)
            value = (symmetric.astype(F32) + dot(inner, edge[level, 2])).astype(BF16)
            put_rows(refined, g, value)
            sums = total[...]
            for i in range(BPC):
                sums += dot(onehot[g * BPC + i], value[i * BLK : (i + 1) * BLK])
            total[...] = sums

        loop(N_SRC, listen)
        part[...] = total[...].astype(BF16).reshape(part.shape)
        for half in range(HALVES):
            for hop in (4, 3, 5, 2, 6, 1, 7, 0):
                t = (s + hop) % N_SRC
                td = ((z + t // 2 + 2 * (t % 2)) % 4) * 4 + y

                @pl.when((t != s) | (td != d))
                def _():
                    remote(
                        part.at[half, t],
                        gathered.at[half, s],
                        part_send,
                        part_recv.at[half],
                        t,
                        td,
                    ).start()

        def ahead(g):
            base[span(g), :] = dot(rows_of(refined, g), edge[level, 3])

        loop(N_SRC, ahead)
        home = ((z + 8 - x - 2 * core) % 4) * 4 + y
        total[...] = jnp.zeros_like(total)
        drain(arr.at[pl.ds(0, DEVS - 1)], msg_send)

        near = home // 2
        slot = home % 2
        for half in range(HALVES):

            @pl.when(home == d)
            def _():
                gathered[half, pl.ds(s, 1)] = part[half, pl.ds(s, 1)]
                drain(gathered.at[half, pl.ds(0, N_SRC - 1)], part_recv.at[half])

            @pl.when(home != d)
            def _():
                drain(gathered.at[half], part_recv.at[half])

            sums = gathered[half, 0].astype(F32)
            for i in range(1, N_SRC):
                sums += gathered[half, i].astype(F32)
            sums = (sums * DEGREE ** (-0.5)).astype(BF16)
            sums = dot(sums, edge[level, 3]).astype(BF16)
            atoms[half] = sums

            @pl.when(near == s)
            def _():
                region[pl.ds(slot, 1), half, pl.ds(s, 1)] = sums[None, None]

            for far in FAR:
                t = ((z + far[0]) % 4) * 4 + (y + far[1]) % 4

                @pl.when(near * N_DST + t != me)
                def _():
                    remote(
                        atoms.at[half],
                        region.at[slot, half, s],
                        atom_send,
                        atom_recv,
                        near,
                        t,
                    ).start()

        @pl.when(home == d)
        def _():
            drain(gathered.at[0], part_send)
            drain(gathered.at[1, pl.ds(0, N_SRC - 2)], part_send)

        @pl.when(home != d)
        def _():
            drain(gathered, part_send)

        @pl.when(near == s)
        def _():
            drain(arr.at[pl.ds(0, 2 * (N_DST - 1))], atom_recv)
            drain(arr.at[pl.ds(0, 2 * (N_DST - 1))], atom_send)

        @pl.when(near != s)
        def _():
            drain(arr.at[pl.ds(0, 2 * N_DST)], atom_recv)
            drain(arr.at[pl.ds(0, 2 * N_DST)], atom_send)

        def update(g):
            chosen = pick[pl.ds(g * WIDE * BPC, WIDE * BPC)]
            chosen = chosen.reshape(WIDE * CHUNK, 2 * ATOM_ROWS)
            feed = dot(chosen, region[...].reshape(2 * ATOM_ROWS, WIDTH))
            first = silu_of_half(base[span(g, WIDE), :] + feed).astype(BF16)
            second = silu_of_half(dot(first, edge[level, 4])).astype(BF16)
            fresh = (
                rows_of(state, g, WIDE).astype(F32)
                + rows_of(refined, g, WIDE).astype(F32)
                + dot(second, edge[level, 5])
            )
            fresh = (fresh * (live_of(g, WIDE) * 0.5**0.5)).astype(BF16)
            put_rows(state, g, fresh, WIDE)

            @pl.when(level < NBLK - 1)
            def _():
                lower(level + 1, g, fresh)
                share(g * WIDE, WIDE)

        loop(N_SRC // WIDE, update)

        @pl.when(level < NBLK - 1)
        def _():
            loop(N_SRC, lambda g: base_of(level + 1, g))

    loop(NBLK, run_level)


def body(
    edge_state, directions, src_atom, dst_atom, rev_pos, counts, triplets, down_w, trip_w, edge_w
):
    vmem = pl.BlockSpec(memory_space=pltpu.VMEM)
    hbm = pl.BlockSpec(memory_space=pl.ANY)
    dma = pltpu.SemaphoreType.DMA
    down = jnp.swapaxes(down_w, 1, 2)
    edges = pltpu.VMEM((DEVS, CAP, WIDTH), BF16)
    out = pl.pallas_call(
        kernel,
        out_shape=pltpu.VMEM((DEVS, CAP, WIDTH), BF16),
        in_specs=[pl.BlockSpec(memory_space=pltpu.SMEM)] + [vmem] * 5 + [hbm] * 4,
        out_specs=vmem,
        scratch_shapes=[
            pltpu.VMEM((ROWS, WIDTH), F32),
            edges,
            edges,
            edges,
            pltpu.VMEM((NBLOCK, 8, BLK), F32),
            pltpu.VMEM((NBLOCK, HPAD, BLK), F32),
            pltpu.VMEM((NBLOCK, HPAD, BLK), BF16),
            pltpu.VMEM((NBLOCK, BLK, HPAD), F32),
            pltpu.VMEM((N_SRC * N_SRC, HARM, 2 * TRIP), BF16),
            pltpu.VMEM((NBLOCK, HPAD, 4 * TRIP), BF16),
            pltpu.VMEM((NBLOCK, HPAD, WIDTH), BF16),
            pltpu.VMEM((NBLOCK, ATOM_ROWS, BLK), BF16),
            pltpu.VMEM((NBLOCK, BLK, BLK), BF16),
            pltpu.VMEM((NBLOCK, BLK, 2 * ATOM_ROWS), BF16),
            pltpu.VMEM(down.shape, BF16),
            pltpu.VMEM(trip_w.shape, BF16),
            pltpu.VMEM(edge_w.shape, BF16),
            pltpu.VMEM((ATOM_ROWS, WIDTH), F32),
            pltpu.VMEM((HALVES, N_SRC, PIECE, WIDTH), BF16),
            pltpu.VMEM((HALVES, N_SRC, PIECE, WIDTH), BF16),
            pltpu.VMEM((HALVES, PIECE, WIDTH), BF16),
            pltpu.VMEM((2, HALVES, N_SRC, PIECE, WIDTH), BF16),
            dma((4,)),
            dma,
            dma((N_SRC,)),
            dma,
            dma((N_SRC,)),
            dma,
            dma((HALVES,)),
            dma,
            dma,
        ],
        compiler_params=pltpu.CompilerParams(
            collective_id=0, has_side_effects=True, vmem_limit_bytes=60 << 20
        ),
    )(
        triplets.T,
        directions,
        src_atom.reshape(NBLOCK, BLK),
        dst_atom.reshape(NBLOCK, BLK),
        rev_pos.reshape(NBLOCK, BLK),
        counts,
        edge_state.reshape(DEVS, CAP, WIDTH),
        down,
        trip_w,
        edge_w,
    )
    return out.reshape(ROWS, WIDTH)


def solution(mesh):
    placed = (
        P(("src", "dst"), None),
        P(None, ("src", "dst")),
        P(("src", "dst")),
        P(("src", "dst")),
        P(("src", "dst")),
        P(("src", "dst"), None),
        P(("src", "dst"), None),
        P(),
        P(),
        P(),
    )
    return jax.shard_map(
        body, mesh=mesh, in_specs=placed, out_specs=P(("src", "dst"), None), check_vma=False
    )
```

```python
import jax
import jax.numpy as jnp
from jax import lax
from jax.experimental import pallas as pl
from jax.experimental.pallas import tpu as pltpu
from jax.sharding import PartitionSpec as P

BLK = 128
PAIRS = 4
NBLK = 2
HARM = 24
HPAD = 32
TRIP = 64
DEGREE = 64
N_SRC = 8
N_DST = 16
DEVS = N_SRC * N_DST
CAP = 16
WIDTH = 512
ROWS = DEVS * CAP
CHUNK = N_DST * CAP
NBLOCK = ROWS // BLK
BPC = CHUNK // BLK
MIX = 4
WIDE = 4
ATOM_ROWS = 256
HALVES = 2
PIECE = ATOM_ROWS // N_SRC // HALVES
FAR = sorted(
    ((i, j) for i in range(4) for j in range(4)),
    key=lambda p: -min(p[0], 4 - p[0]) - min(p[1], 4 - p[1]),
)
MESH = pl.DeviceIdType.MESH
F32 = jnp.float32
BF16 = jnp.bfloat16


def silu_of_half(half):
    return half + half * jnp.tanh(half)


def dot(a, b):
    return jnp.dot(a, b, preferred_element_type=F32)


def loop(count, step):
    def body(i, carry):
        step(i)
        return carry

    lax.fori_loop(0, count, body, 0)


def harmonics(x, y, z):
    xx, yy, zz = x * x, y * y, z * z
    diff = xx - yy
    r3, r5, r15, r35 = 3.0**0.5, 5.0**0.5, 15.0**0.5, 35.0**0.5
    r38, r58, r358 = 0.375**0.5, 0.625**0.5, 4.375**0.5
    return [
        x,
        y,
        z,
        r3 * x * y,
        r3 * y * z,
        r3 * x * z,
        0.5 * r3 * diff,
        1.5 * zz - 0.5,
        r58 * y * (3.0 * xx - yy),
        r15 * x * y * z,
        r38 * y * (5.0 * zz - 1.0),
        0.5 * z * (5.0 * zz - 3.0),
        r38 * x * (5.0 * zz - 1.0),
        0.5 * r15 * z * diff,
        r58 * x * (xx - 3.0 * yy),
        0.5 * r35 * x * y * diff,
        r358 * y * z * (3.0 * xx - yy),
        0.5 * r5 * x * y * (7.0 * zz - 1.0),
        r58 * y * z * (7.0 * zz - 3.0),
        0.125 * (35.0 * zz * zz - 30.0 * zz + 3.0),
        r58 * x * z * (7.0 * zz - 3.0),
        0.25 * r5 * diff * (7.0 * zz - 1.0),
        r358 * x * z * (xx - 3.0 * yy),
        0.125 * r35 * (xx * xx - 6.0 * xx * yy + yy * yy),
    ]


def kernel(
    tri,
    dirs_in,
    src_in,
    dst_in,
    rev_in,
    counts_in,
    state_in,
    down_in,
    trip_in,
    edge_in,
    state,
    base,
    msg,
    arr,
    refined,
    split,
    field,
    rows_y,
    cols,
    pool,
    spectrum,
    lifted,
    onehot,
    mirror,
    pick,
    down,
    trip,
    edge,
    total,
    part,
    gathered,
    atoms,
    region,
    load_sem,
    pool_send,
    pool_recv,
    msg_send,
    msg_recv,
    part_send,
    part_recv,
    atom_send,
    atom_recv,
):
    s = lax.axis_index("src")
    d = lax.axis_index("dst")
    me = s * N_DST + d
    x = s // 2
    core = s % 2
    z = d // 4
    y = d % 4

    def remote(src, dst, send, recv, ts, td):
        return pltpu.make_async_remote_copy(
            src_ref=src,
            dst_ref=dst,
            send_sem=send,
            recv_sem=recv,
            device_id=(ts, td),
            device_id_type=MESH,
        )

    def drain(ref, sem):
        pltpu.make_async_copy(ref, ref, sem).wait()

    barrier = pltpu.get_barrier_semaphore()

    loads = [
        pltpu.make_async_copy(a, b, load_sem.at[i])
        for i, (a, b) in enumerate(
            [(state_in, state), (down_in, down), (edge_in, edge), (trip_in, trip)]
        )
    ]
    for load in loads:
        load.start()
    def signal(ts, td):
        pl.semaphore_signal(barrier, inc=1, device_id=(ts, td), device_id_type=MESH)

    lines = [lax.rem(s + hop, N_SRC) for hop in range(N_SRC)]
    stacks = [lax.rem(z + hop, 4) * 4 for hop in range(4)]
    rows = [lax.rem(y + hop, 4) for hop in range(4)]

    for far in FAR[:-1]:
        for ts in lines:
            signal(ts, stacks[far[0]] + rows[far[1]])
    for ts in lines[1:]:
        signal(ts, d)
    total[...] = jnp.zeros_like(total)
    arr[pl.ds(me, 1)] = jnp.zeros((1, CAP, WIDTH), BF16)

    def iota(shape, axis):
        return lax.broadcasted_iota(jnp.int32, shape, axis)

    lane = iota((NBLOCK, BLK), 1)
    number = iota((NBLOCK, BLK), 0)
    spread_counts = jnp.where(
        lane // (BLK // CAP) == number,
        jnp.broadcast_to(counts_in[...], (NBLOCK, BLK)),
        0,
    ).astype(F32)
    widen = iota((BLK, BLK), 0) % (BLK // CAP) == iota((BLK, BLK), 1) // CAP
    filled = dot(spread_counts.astype(BF16), widen.astype(F32).astype(BF16))
    slot = lane % CAP
    for c in range(NBLOCK):
        split[c, 0:3, :] = dirs_in[:, c * BLK : (c + 1) * BLK]
    field[...] = jnp.zeros_like(field)
    planes = harmonics(split[:, 0, :], split[:, 1, :], split[:, 2, :])
    for i, plane in enumerate(planes):
        field[:, i, :] = plane
    live = (slot.astype(F32) < filled).astype(F32)
    rows_y[...] = (field[...] * live[:, None, :]).astype(BF16)
    field[:, HARM, :] = live
    field[:, HARM + 1, :] = src_in[...].astype(F32)
    field[:, HARM + 2, :] = (lane - slot + rev_in[...]).astype(F32)

    def turn(c):
        cols[c] = field[c].T

    def rows_of(ref, g, n=1):
        return ref[pl.ds(g * n * N_DST, n * N_DST)].reshape(n * CHUNK, WIDTH)

    def put_rows(ref, g, value, n=1):
        ref[pl.ds(g * n * N_DST, n * N_DST)] = value.reshape(n * N_DST, CAP, WIDTH)

    def live_of(g, n=1):
        column = cols[pl.ds(g * n * BPC, n * BPC), :, HARM : HARM + 1]
        return column.reshape(n * CHUNK, 1)

    def lower(level, g, value):
        n = value.shape[0] // CHUNK
        low = lax.dot_general(
            value, down[level], (((1,), (1,)), ((), ())), preferred_element_type=F32
        )
        low = silu_of_half(low).astype(BF16)
        modes = []
        for i in range(n * BPC):
            c = g * n * BPC + i
            modes.append(dot(rows_y[c], low[i * BLK : (i + 1) * BLK])[:HARM])
        for i in range(n):
            pool[s * N_SRC + g * n + i] = jnp.concatenate(
                [modes[2 * i], modes[2 * i + 1]], axis=1
            ).astype(BF16)

    def share(start, count):
        piece = pool.at[pl.ds(s * N_SRC + start, count)]
        for hop in range(1, N_SRC):
            remote(
                piece, piece, pool_send, pool_recv.at[s], (s + hop) % N_SRC, d
            ).start()

    def span(g, n=1):
        return pl.ds(pl.multiple_of(g * n * CHUNK, CHUNK), n * CHUNK)

    def base_of(level, g):
        base[span(g), :] = dot(rows_of(state, g), edge[level, 0])

    loads[0].wait()
    loads[1].wait()
    down[...] = down[...] * 0.5
    loop(N_SRC // WIDE, lambda g: lower(0, g, rows_of(state, g, WIDE)))
    pl.semaphore_wait(barrier, DEVS - 1)
    share(0, N_SRC)

    place = iota((BLK, 2 * ATOM_ROWS), 1)
    group = ATOM_ROWS // HALVES
    half_of = place // (2 * group)
    slot_of = place // group - 2 * half_of
    atom_of = (slot_of * ATOM_ROWS + half_of * group + place % group).astype(F32)

    def choose(c):
        column = cols[c]
        source = column[:, HARM + 1 : HARM + 2]
        target = column[:, HARM + 2 : HARM + 3]
        alive = column[:, HARM : HARM + 1]
        pick[c] = (source == atom_of).astype(F32).astype(BF16)
        same = (target == iota((BLK, BLK), 1).astype(F32)).astype(F32)
        mirror[c] = (same * alive).astype(BF16)
        half = pl.ds(pl.multiple_of(lax.rem(c, BPC) * BLK, BLK), BLK)
        onehot[lax.div(c, BPC), :, half] = (
            (iota((ATOM_ROWS, BLK), 0) == dst_in[pl.ds(c, 1), :]).astype(F32).astype(BF16)
        )

    loop(NBLOCK, turn)
    loop(NBLOCK, choose)

    def halve(level):
        for i in (0, 1, 3, 4):
            edge[level, i] = edge[level, i] * 0.5

    loads[2].wait()
    loop(NBLK, halve)
    loop(N_SRC, lambda g: base_of(0, g))
    loads[3].wait()
    mode = iota((HARM, 4 * TRIP), 0)
    degree = (
        (mode >= 3).astype(jnp.int32)
        + (mode >= 8).astype(jnp.int32)
        + (mode >= 15).astype(jnp.int32)
    )
    keep = (degree == iota((HARM, 4 * TRIP), 1) // TRIP).astype(F32) * (0.5 * (BLK * PAIRS) ** (-0.5))

    side = iota((HARM, 2 * TRIP), 1) // TRIP

    def run_level(level):
        drain(pool.at[pl.ds(0, (N_SRC - 1) * N_SRC)], pool_send)
        for hop in range(1, N_SRC):
            owner = (s + hop) % N_SRC
            drain(pool.at[pl.ds(owner * N_SRC, N_SRC)], pool_recv.at[owner])

        def mix(i):
            mixed = []
            for k in range(MIX):
                c = i * MIX + k
                modes = []
                for q in range(PAIRS):
                    block = pool[lax.div(tri[q, c], 2)].astype(F32)
                    wanted = side == lax.rem(tri[q, c], 2)
                    modes.append(jnp.where(wanted, block, 0.0))
                modes = (modes[0] + modes[1]) + (modes[2] + modes[3])
                modes = modes + pltpu.roll(modes, TRIP, 1)
                modes = jnp.concatenate([modes, modes], axis=1) * keep
                modes = jnp.concatenate([modes, jnp.zeros((HPAD - HARM, 4 * TRIP), F32)], axis=0)
                mixed.append(modes.astype(BF16))
            spectrum[pl.ds(i * MIX, MIX)] = jnp.stack(mixed)

        loop(NBLOCK // MIX, mix)
        lifted[...] = (
            dot(spectrum[...].reshape(NBLOCK * HPAD, 4 * TRIP), trip[level])
            .astype(BF16)
            .reshape(NBLOCK, HPAD, WIDTH)
        )

        def talk(j):
            g = (s + 3 + 3 * j) % N_SRC
            parts = [
                dot(cols[g * BPC + i].astype(BF16), lifted[g * BPC + i]) for i in range(BPC)
            ]
            pre = base[span(g), :] + jnp.concatenate(parts, axis=0)
            put_rows(msg, g, (silu_of_half(pre) * live_of(g)).astype(BF16))

            def send(i):
                row = lax.rem(y + i + 2, 4)
                for k in range(4):
                    t = stacks[(k + 2) % 4] + row
                    b = g * N_DST + t

                    @pl.when(b != me)
                    def _():
                        remote(msg.at[b], arr.at[me], msg_send, msg_recv.at[s], g, t).start()

            loop(N_DST // 4, send)

        loop(N_SRC, talk)

        def arrived(g):
            @pl.when(g != s)
            def _():
                drain(arr.at[pl.ds(g * N_DST, N_DST)], msg_recv.at[g])

            @pl.when(g == s)
            def _():
                drain(arr.at[pl.ds(0, N_DST - 1)], msg_recv.at[g])

        def listen(j):
            chunks = [(s + 4 * N_SRC - 3 - 3 * (2 * j + k)) % N_SRC for k in range(2)]
            for g in chunks:
                arrived(g)
            mirrored = []
            for g in chunks:
                came = rows_of(arr, g)
                for i in range(BPC):
                    mirrored.append(dot(mirror[g * BPC + i], came[i * BLK : (i + 1) * BLK]))
            own = jnp.concatenate([rows_of(msg, g) for g in chunks], axis=0)
            symmetric = (own.astype(F32) + jnp.concatenate(mirrored, axis=0)).astype(BF16)
            inner = silu_of_half(dot(symmetric, edge[level, 1])).astype(BF16)
            value = (symmetric.astype(F32) + dot(inner, edge[level, 2])).astype(BF16)
            hits = jnp.concatenate([onehot[g] for g in chunks], axis=1)
            total[...] += dot(hits, value)
            for k in range(2):
                put_rows(refined, chunks[k], value[k * CHUNK : (k + 1) * CHUNK])

        loop(N_SRC // 2, listen)
        part[...] = total[...].astype(BF16).reshape(part.shape)
        for half in range(HALVES):
            for hop in (4, 3, 5, 2, 6, 1, 7, 0):
                t = lines[hop]
                td = lax.rem(z + lax.div(t, 2) + 2 * lax.rem(t, 2), 4) * 4 + y

                @pl.when((t != s) | (td != d))
                def _():
                    remote(
                        part.at[half, t],
                        gathered.at[half, s],
                        part_send,
                        part_recv.at[half],
                        t,
                        td,
                    ).start()

        def ahead(g):
            base[span(g), :] = dot(rows_of(refined, g), edge[level, 3])

        loop(N_SRC, ahead)
        home = ((z + 8 - x - 2 * core) % 4) * 4 + y
        total[...] = jnp.zeros_like(total)
        drain(arr.at[pl.ds(0, DEVS - 1)], msg_send)

        near = home // 2
        slot = home % 2
        for half in range(HALVES):

            @pl.when(home == d)
            def _():
                gathered[half, pl.ds(s, 1)] = part[half, pl.ds(s, 1)]
                drain(gathered.at[half, pl.ds(0, N_SRC - 1)], part_recv.at[half])

            @pl.when(home != d)
            def _():
                drain(gathered.at[half], part_recv.at[half])

            sums = gathered[half, 0].astype(F32)
            for i in range(1, N_SRC):
                sums += gathered[half, i].astype(F32)
            sums = (sums * DEGREE ** (-0.5)).astype(BF16)
            sums = dot(sums, edge[level, 3]).astype(BF16)
            atoms[half] = sums

            @pl.when(near == s)
            def _():
                region[half, pl.ds(slot, 1), pl.ds(s, 1)] = sums[None, None]

            for far in FAR:
                t = stacks[far[0]] + rows[far[1]]

                @pl.when(near * N_DST + t != me)
                def _():
                    remote(
                        atoms.at[half],
                        region.at[half, slot, s],
                        atom_send.at[half],
                        atom_recv.at[half],
                        near,
                        t,
                    ).start()

        @pl.when(home == d)
        def _():
            drain(gathered.at[0], part_send)
            drain(gathered.at[1, pl.ds(0, N_SRC - 2)], part_send)

        @pl.when(home != d)
        def _():
            drain(gathered, part_send)

        def feed_of(half, g):
            columns = pick[pl.ds(g * WIDE * BPC, WIDE * BPC), :, half * ATOM_ROWS : (half + 1) * ATOM_ROWS]
            return dot(
                columns.reshape(WIDE * CHUNK, ATOM_ROWS),
                region[half].reshape(ATOM_ROWS, WIDTH),
            )

        def await_half(half):
            @pl.when(near == s)
            def _():
                drain(arr.at[pl.ds(0, N_DST - 1)], atom_recv.at[half])
                drain(arr.at[pl.ds(0, N_DST - 1)], atom_send.at[half])

            @pl.when(near != s)
            def _():
                drain(arr.at[pl.ds(0, N_DST)], atom_recv.at[half])
                drain(arr.at[pl.ds(0, N_DST)], atom_send.at[half])

        def early(g):
            base[span(g, WIDE), :] += feed_of(0, g)

        await_half(0)
        loop(N_SRC // WIDE, early)
        await_half(1)

        def update(g):
            first = silu_of_half(base[span(g, WIDE), :] + feed_of(1, g)).astype(BF16)
            second = silu_of_half(dot(first, edge[level, 4])).astype(BF16)
            fresh = (
                rows_of(state, g, WIDE).astype(F32)
                + rows_of(refined, g, WIDE).astype(F32)
                + dot(second, edge[level, 5])
            )
            fresh = (fresh * (live_of(g, WIDE) * 0.5**0.5)).astype(BF16)
            put_rows(state, g, fresh, WIDE)

            @pl.when(level < NBLK - 1)
            def _():
                for k in range(2):
                    lower(level + 1, 2 * g + k, rows_of(state, 2 * g + k, WIDE // 2))
                    share(g * WIDE + k * WIDE // 2, WIDE // 2)

        loop(N_SRC // WIDE, update)

        @pl.when(level < NBLK - 1)
        def _():
            loop(N_SRC, lambda g: base_of(level + 1, g))

    loop(NBLK, run_level)


def body(
    edge_state, directions, src_atom, dst_atom, rev_pos, counts, triplets, down_w, trip_w, edge_w
):
    vmem = pl.BlockSpec(memory_space=pltpu.VMEM)
    hbm = pl.BlockSpec(memory_space=pl.ANY)
    dma = pltpu.SemaphoreType.DMA
    down = jnp.swapaxes(down_w, 1, 2)
    edges = pltpu.VMEM((DEVS, CAP, WIDTH), BF16)
    out = pl.pallas_call(
        kernel,
        out_shape=pltpu.VMEM((DEVS, CAP, WIDTH), BF16),
        in_specs=[pl.BlockSpec(memory_space=pltpu.SMEM)] + [vmem] * 5 + [hbm] * 4,
        out_specs=vmem,
        scratch_shapes=[
            pltpu.VMEM((ROWS, WIDTH), F32),
            edges,
            edges,
            edges,
            pltpu.VMEM((NBLOCK, 8, BLK), F32),
            pltpu.VMEM((NBLOCK, HPAD, BLK), F32),
            pltpu.VMEM((NBLOCK, HPAD, BLK), BF16),
            pltpu.VMEM((NBLOCK, BLK, HPAD), F32),
            pltpu.VMEM((N_SRC * N_SRC, HARM, 2 * TRIP), BF16),
            pltpu.VMEM((NBLOCK, HPAD, 4 * TRIP), BF16),
            pltpu.VMEM((NBLOCK, HPAD, WIDTH), BF16),
            pltpu.VMEM((N_SRC, ATOM_ROWS, CHUNK), BF16),
            pltpu.VMEM((NBLOCK, BLK, BLK), BF16),
            pltpu.VMEM((NBLOCK, BLK, 2 * ATOM_ROWS), BF16),
            pltpu.VMEM(down.shape, BF16),
            pltpu.VMEM(trip_w.shape, BF16),
            pltpu.VMEM(edge_w.shape, BF16),
            pltpu.VMEM((ATOM_ROWS, WIDTH), F32),
            pltpu.VMEM((HALVES, N_SRC, PIECE, WIDTH), BF16),
            pltpu.VMEM((HALVES, N_SRC, PIECE, WIDTH), BF16),
            pltpu.VMEM((HALVES, PIECE, WIDTH), BF16),
            pltpu.VMEM((HALVES, 2, N_SRC, PIECE, WIDTH), BF16),
            dma((4,)),
            dma,
            dma((N_SRC,)),
            dma,
            dma((N_SRC,)),
            dma,
            dma((HALVES,)),
            dma((HALVES,)),
            dma((HALVES,)),
        ],
        compiler_params=pltpu.CompilerParams(
            collective_id=0, has_side_effects=True, vmem_limit_bytes=60 << 20
        ),
    )(
        triplets.T,
        directions,
        src_atom.reshape(NBLOCK, BLK),
        dst_atom.reshape(NBLOCK, BLK),
        rev_pos.reshape(NBLOCK, BLK),
        counts,
        edge_state.reshape(DEVS, CAP, WIDTH),
        down,
        trip_w,
        edge_w,
    )
    return out.reshape(ROWS, WIDTH)


def solution(mesh):
    placed = (
        P(("src", "dst"), None),
        P(None, ("src", "dst")),
        P(("src", "dst")),
        P(("src", "dst")),
        P(("src", "dst")),
        P(("src", "dst"), None),
        P(("src", "dst"), None),
        P(),
        P(),
        P(),
    )
    return jax.shard_map(
        body, mesh=mesh, in_specs=placed, out_specs=P(("src", "dst"), None), check_vma=False
    )
```

```python
import jax
import jax.numpy as jnp
from jax import lax
from jax.experimental import pallas as pl
from jax.experimental.pallas import tpu as pltpu
from jax.sharding import PartitionSpec as P

BLK = 128
PAIRS = 4
NBLK = 2
HARM = 24
HPAD = 32
TRIP = 64
DEGREE = 64
N_SRC = 8
N_DST = 16
DEVS = N_SRC * N_DST
CAP = 16
WIDTH = 512
ROWS = DEVS * CAP
CHUNK = N_DST * CAP
NBLOCK = ROWS // BLK
BPC = CHUNK // BLK
MIX = 16
WIDE = 4
ATOM_ROWS = 256
HALVES = 2
PIECE = ATOM_ROWS // N_SRC // HALVES
FAR = sorted(
    ((i, j) for i in range(4) for j in range(4)),
    key=lambda p: -min(p[0], 4 - p[0]) - min(p[1], 4 - p[1]),
)
MESH = pl.DeviceIdType.MESH
F32 = jnp.float32
BF16 = jnp.bfloat16


def silu_of_half(half):
    return half + half * jnp.tanh(half)


def dot(a, b):
    return jnp.dot(a, b, preferred_element_type=F32)


def loop(count, step):
    def body(i, carry):
        step(i)
        return carry

    lax.fori_loop(0, count, body, 0)


def harmonics(x, y, z):
    xx, yy, zz = x * x, y * y, z * z
    diff = xx - yy
    r3, r5, r15, r35 = 3.0**0.5, 5.0**0.5, 15.0**0.5, 35.0**0.5
    r38, r58, r358 = 0.375**0.5, 0.625**0.5, 4.375**0.5
    return [
        x,
        y,
        z,
        r3 * x * y,
        r3 * y * z,
        r3 * x * z,
        0.5 * r3 * diff,
        1.5 * zz - 0.5,
        r58 * y * (3.0 * xx - yy),
        r15 * x * y * z,
        r38 * y * (5.0 * zz - 1.0),
        0.5 * z * (5.0 * zz - 3.0),
        r38 * x * (5.0 * zz - 1.0),
        0.5 * r15 * z * diff,
        r58 * x * (xx - 3.0 * yy),
        0.5 * r35 * x * y * diff,
        r358 * y * z * (3.0 * xx - yy),
        0.5 * r5 * x * y * (7.0 * zz - 1.0),
        r58 * y * z * (7.0 * zz - 3.0),
        0.125 * (35.0 * zz * zz - 30.0 * zz + 3.0),
        r58 * x * z * (7.0 * zz - 3.0),
        0.25 * r5 * diff * (7.0 * zz - 1.0),
        r358 * x * z * (xx - 3.0 * yy),
        0.125 * r35 * (xx * xx - 6.0 * xx * yy + yy * yy),
    ]


def kernel(
    tri,
    dirs_in,
    src_in,
    dst_in,
    rev_in,
    counts_in,
    state_in,
    down_in,
    trip_in,
    edge_in,
    state,
    base,
    msg,
    arr,
    refined,
    split,
    field,
    rows_y,
    cols,
    pool,
    spectrum,
    lifted,
    onehot,
    mirror,
    pick,
    down,
    trip,
    edge,
    total,
    part,
    gathered,
    atoms,
    region,
    load_sem,
    pool_send,
    pool_recv,
    msg_send,
    msg_recv,
    part_send,
    part_recv,
    atom_send,
    atom_recv,
):
    s = lax.axis_index("src")
    d = lax.axis_index("dst")
    me = s * N_DST + d
    x = s // 2
    core = s % 2
    z = d // 4
    y = d % 4

    def remote(src, dst, send, recv, ts, td):
        return pltpu.make_async_remote_copy(
            src_ref=src,
            dst_ref=dst,
            send_sem=send,
            recv_sem=recv,
            device_id=(ts, td),
            device_id_type=MESH,
        )

    def drain(ref, sem):
        pltpu.make_async_copy(ref, ref, sem).wait()

    barrier = pltpu.get_barrier_semaphore()

    loads = [
        pltpu.make_async_copy(a, b, load_sem.at[i])
        for i, (a, b) in enumerate(
            [(state_in, state), (down_in, down), (edge_in, edge), (trip_in, trip)]
        )
    ]
    for load in loads:
        load.start()
    def signal(ts, td):
        pl.semaphore_signal(barrier, inc=1, device_id=(ts, td), device_id_type=MESH)

    lines = [lax.rem(s + hop, N_SRC) for hop in range(N_SRC)]
    stacks = [lax.rem(z + hop, 4) * 4 for hop in range(4)]
    rows = [lax.rem(y + hop, 4) for hop in range(4)]

    for far in FAR[:-1]:
        for ts in lines:
            signal(ts, stacks[far[0]] + rows[far[1]])
    for ts in lines[1:]:
        signal(ts, d)
    total[...] = jnp.zeros_like(total)
    arr[pl.ds(me, 1)] = jnp.zeros((1, CAP, WIDTH), BF16)

    def iota(shape, axis):
        return lax.broadcasted_iota(jnp.int32, shape, axis)

    lane = iota((NBLOCK, BLK), 1)
    number = iota((NBLOCK, BLK), 0)
    spread_counts = jnp.where(
        lane // (BLK // CAP) == number,
        jnp.broadcast_to(counts_in[...], (NBLOCK, BLK)),
        0,
    ).astype(F32)
    widen = iota((BLK, BLK), 0) % (BLK // CAP) == iota((BLK, BLK), 1) // CAP
    filled = dot(spread_counts.astype(BF16), widen.astype(F32).astype(BF16))
    slot = lane % CAP
    for c in range(NBLOCK):
        split[c, 0:3, :] = dirs_in[:, c * BLK : (c + 1) * BLK]
    field[...] = jnp.zeros_like(field)
    planes = harmonics(split[:, 0, :], split[:, 1, :], split[:, 2, :])
    for i, plane in enumerate(planes):
        field[:, i, :] = plane
    live = (slot.astype(F32) < filled).astype(F32)
    rows_y[...] = (field[...] * live[:, None, :]).astype(BF16)
    field[:, HARM, :] = live
    field[:, HARM + 1, :] = src_in[...].astype(F32)
    field[:, HARM + 2, :] = (lane - slot + rev_in[...]).astype(F32)

    def turn(c):
        cols[c] = field[c].T

    def rows_of(ref, g, n=1):
        return ref[pl.ds(g * n * N_DST, n * N_DST)].reshape(n * CHUNK, WIDTH)

    def put_rows(ref, g, value, n=1):
        ref[pl.ds(g * n * N_DST, n * N_DST)] = value.reshape(n * N_DST, CAP, WIDTH)

    def live_of(g, n=1):
        column = cols[pl.ds(g * n * BPC, n * BPC), :, HARM : HARM + 1]
        return column.reshape(n * CHUNK, 1)

    def lower(level, g, value):
        n = value.shape[0] // CHUNK
        low = lax.dot_general(
            value, down[level], (((1,), (1,)), ((), ())), preferred_element_type=F32
        )
        low = silu_of_half(low).astype(BF16)
        modes = []
        for i in range(n * BPC):
            c = g * n * BPC + i
            modes.append(dot(rows_y[c], low[i * BLK : (i + 1) * BLK])[:HARM])
        for i in range(n):
            pool[s * N_SRC + g * n + i] = jnp.concatenate(
                [modes[2 * i], modes[2 * i + 1]], axis=1
            ).astype(BF16)

    def share(start, count):
        piece = pool.at[pl.ds(s * N_SRC + start, count)]
        for hop in range(1, N_SRC):
            remote(
                piece, piece, pool_send, pool_recv.at[s], (s + hop) % N_SRC, d
            ).start()

    def span(g, n=1):
        return pl.ds(pl.multiple_of(g * n * CHUNK, CHUNK), n * CHUNK)

    def base_of(level, g):
        base[span(g), :] = dot(rows_of(state, g), edge[level, 0])

    loads[0].wait()
    loads[1].wait()
    down[...] = down[...] * 0.5
    loop(N_SRC // WIDE, lambda g: lower(0, g, rows_of(state, g, WIDE)))
    pl.semaphore_wait(barrier, DEVS - 1)
    share(0, N_SRC)

    place = iota((BLK, 2 * ATOM_ROWS), 1)
    group = ATOM_ROWS // HALVES
    half_of = place // (2 * group)
    slot_of = place // group - 2 * half_of
    atom_of = (slot_of * ATOM_ROWS + half_of * group + place % group).astype(F32)

    def choose(c):
        column = cols[c]
        source = column[:, HARM + 1 : HARM + 2]
        target = column[:, HARM + 2 : HARM + 3]
        alive = column[:, HARM : HARM + 1]
        pick[c] = (source == atom_of).astype(F32).astype(BF16)
        same = (target == iota((BLK, BLK), 1).astype(F32)).astype(F32)
        mirror[c] = (same * alive).astype(BF16)
        half = pl.ds(pl.multiple_of(lax.rem(c, BPC) * BLK, BLK), BLK)
        onehot[lax.div(c, BPC), :, half] = (
            (iota((ATOM_ROWS, BLK), 0) == dst_in[pl.ds(c, 1), :]).astype(F32).astype(BF16)
        )

    loop(NBLOCK, turn)
    loop(NBLOCK, choose)

    def halve(level):
        for i in (0, 1, 3, 4):
            edge[level, i] = edge[level, i] * 0.5

    loads[2].wait()
    loop(NBLK, halve)
    loop(N_SRC, lambda g: base_of(0, g))
    loads[3].wait()
    mode = iota((HARM, 4 * TRIP), 0)
    degree = (
        (mode >= 3).astype(jnp.int32)
        + (mode >= 8).astype(jnp.int32)
        + (mode >= 15).astype(jnp.int32)
    )
    keep = (degree == iota((HARM, 4 * TRIP), 1) // TRIP).astype(F32) * (0.5 * (BLK * PAIRS) ** (-0.5))

    side = iota((HARM, 2 * TRIP), 1) // TRIP

    def run_level(level):
        drain(pool.at[pl.ds(0, (N_SRC - 1) * N_SRC)], pool_send)
        for hop in range(1, N_SRC):
            owner = (s + hop) % N_SRC
            drain(pool.at[pl.ds(owner * N_SRC, N_SRC)], pool_recv.at[owner])

        def mix(i):
            mixed = []
            for k in range(MIX):
                c = i * MIX + k
                modes = []
                for q in range(PAIRS):
                    block = pool[lax.div(tri[q, c], 2)].astype(F32)
                    wanted = side == lax.rem(tri[q, c], 2)
                    modes.append(jnp.where(wanted, block, 0.0))
                modes = (modes[0] + modes[1]) + (modes[2] + modes[3])
                modes = modes + pltpu.roll(modes, TRIP, 1)
                modes = jnp.concatenate([modes, modes], axis=1) * keep
                modes = jnp.concatenate([modes, jnp.zeros((HPAD - HARM, 4 * TRIP), F32)], axis=0)
                mixed.append(modes.astype(BF16))
            spectrum[pl.ds(i * MIX, MIX)] = jnp.stack(mixed)

        loop(NBLOCK // MIX, mix)
        lifted[...] = (
            dot(spectrum[...].reshape(NBLOCK * HPAD, 4 * TRIP), trip[level])
            .astype(BF16)
            .reshape(NBLOCK, HPAD, WIDTH)
        )

        def talk(j):
            g = (s + 3 + 3 * j) % N_SRC
            parts = [
                dot(cols[g * BPC + i].astype(BF16), lifted[g * BPC + i]) for i in range(BPC)
            ]
            pre = base[span(g), :] + jnp.concatenate(parts, axis=0)
            put_rows(msg, g, (silu_of_half(pre) * live_of(g)).astype(BF16))

            def send(i):
                row = lax.rem(y + i + 2, 4)
                for k in range(4):
                    t = stacks[(k + 2) % 4] + row
                    b = g * N_DST + t

                    @pl.when(b != me)
                    def _():
                        remote(msg.at[b], arr.at[me], msg_send, msg_recv.at[s], g, t).start()

            loop(N_DST // 4, send)

        loop(N_SRC, talk)

        def arrived(g):
            @pl.when(g != s)
            def _():
                drain(arr.at[pl.ds(g * N_DST, N_DST)], msg_recv.at[g])

            @pl.when(g == s)
            def _():
                drain(arr.at[pl.ds(0, N_DST - 1)], msg_recv.at[g])

        def listen(j):
            chunks = [(s + 4 * N_SRC - 3 - 3 * (2 * j + k)) % N_SRC for k in range(2)]
            for g in chunks:
                arrived(g)
            mirrored = []
            for g in chunks:
                came = rows_of(arr, g)
                for i in range(BPC):
                    mirrored.append(dot(mirror[g * BPC + i], came[i * BLK : (i + 1) * BLK]))
            own = jnp.concatenate([rows_of(msg, g) for g in chunks], axis=0)
            symmetric = (own.astype(F32) + jnp.concatenate(mirrored, axis=0)).astype(BF16)
            inner = silu_of_half(dot(symmetric, edge[level, 1])).astype(BF16)
            value = (symmetric.astype(F32) + dot(inner, edge[level, 2])).astype(BF16)
            hits = jnp.concatenate([onehot[g] for g in chunks], axis=1)
            total[...] += dot(hits, value)
            for k in range(2):
                put_rows(refined, chunks[k], value[k * CHUNK : (k + 1) * CHUNK])

        loop(N_SRC // 2, listen)
        part[...] = total[...].astype(BF16).reshape(part.shape)
        for half in range(HALVES):
            for hop in (4, 3, 5, 2, 6, 1, 7, 0):
                t = lines[hop]
                td = lax.rem(z + lax.div(t, 2) + 2 * lax.rem(t, 2), 4) * 4 + y

                @pl.when((t != s) | (td != d))
                def _():
                    remote(
                        part.at[half, t],
                        gathered.at[half, s],
                        part_send,
                        part_recv.at[half],
                        t,
                        td,
                    ).start()

        def ahead(g):
            base[span(g), :] = dot(rows_of(refined, g), edge[level, 3])

        loop(N_SRC, ahead)
        home = ((z + 8 - x - 2 * core) % 4) * 4 + y
        total[...] = jnp.zeros_like(total)
        drain(arr.at[pl.ds(0, DEVS - 1)], msg_send)

        near = home // 2
        slot = home % 2
        for half in range(HALVES):

            @pl.when(home == d)
            def _():
                gathered[half, pl.ds(s, 1)] = part[half, pl.ds(s, 1)]
                drain(gathered.at[half, pl.ds(0, N_SRC - 1)], part_recv.at[half])

            @pl.when(home != d)
            def _():
                drain(gathered.at[half], part_recv.at[half])

            sums = gathered[half, 0].astype(F32)
            for i in range(1, N_SRC):
                sums += gathered[half, i].astype(F32)
            sums = (sums * DEGREE ** (-0.5)).astype(BF16)
            sums = dot(sums, edge[level, 3]).astype(BF16)
            atoms[half] = sums

            @pl.when(near == s)
            def _():
                region[half, pl.ds(slot, 1), pl.ds(s, 1)] = sums[None, None]

            for far in FAR:
                t = stacks[far[0]] + rows[far[1]]

                @pl.when(near * N_DST + t != me)
                def _():
                    remote(
                        atoms.at[half],
                        region.at[half, slot, s],
                        atom_send.at[half],
                        atom_recv.at[half],
                        near,
                        t,
                    ).start()

        @pl.when(home == d)
        def _():
            drain(gathered.at[0], part_send)
            drain(gathered.at[1, pl.ds(0, N_SRC - 2)], part_send)

        @pl.when(home != d)
        def _():
            drain(gathered, part_send)

        def feed_of(half, g):
            columns = pick[pl.ds(g * WIDE * BPC, WIDE * BPC), :, half * ATOM_ROWS : (half + 1) * ATOM_ROWS]
            return dot(
                columns.reshape(WIDE * CHUNK, ATOM_ROWS),
                region[half].reshape(ATOM_ROWS, WIDTH),
            )

        def await_half(half):
            @pl.when(near == s)
            def _():
                drain(arr.at[pl.ds(0, N_DST - 1)], atom_recv.at[half])
                drain(arr.at[pl.ds(0, N_DST - 1)], atom_send.at[half])

            @pl.when(near != s)
            def _():
                drain(arr.at[pl.ds(0, N_DST)], atom_recv.at[half])
                drain(arr.at[pl.ds(0, N_DST)], atom_send.at[half])

        def early(g):
            base[span(g, WIDE), :] += feed_of(0, g)

        await_half(0)
        loop(N_SRC // WIDE, early)
        await_half(1)

        def update(g):
            first = silu_of_half(base[span(g, WIDE), :] + feed_of(1, g)).astype(BF16)
            second = silu_of_half(dot(first, edge[level, 4])).astype(BF16)
            fresh = (
                rows_of(state, g, WIDE).astype(F32)
                + rows_of(refined, g, WIDE).astype(F32)
                + dot(second, edge[level, 5])
            )
            fresh = (fresh * (live_of(g, WIDE) * 0.5**0.5)).astype(BF16)
            put_rows(state, g, fresh, WIDE)

            @pl.when(level < NBLK - 1)
            def _():
                for k in range(2):
                    lower(level + 1, 2 * g + k, rows_of(state, 2 * g + k, WIDE // 2))
                    share(g * WIDE + k * WIDE // 2, WIDE // 2)

        loop(N_SRC // WIDE, update)

        @pl.when(level < NBLK - 1)
        def _():
            loop(N_SRC, lambda g: base_of(level + 1, g))

    loop(NBLK, run_level)


def body(
    edge_state, directions, src_atom, dst_atom, rev_pos, counts, triplets, down_w, trip_w, edge_w
):
    vmem = pl.BlockSpec(memory_space=pltpu.VMEM)
    hbm = pl.BlockSpec(memory_space=pl.ANY)
    dma = pltpu.SemaphoreType.DMA
    down = jnp.swapaxes(down_w, 1, 2)
    edges = pltpu.VMEM((DEVS, CAP, WIDTH), BF16)
    out = pl.pallas_call(
        kernel,
        out_shape=pltpu.VMEM((DEVS, CAP, WIDTH), BF16),
        in_specs=[pl.BlockSpec(memory_space=pltpu.SMEM)] + [vmem] * 5 + [hbm] * 4,
        out_specs=vmem,
        scratch_shapes=[
            pltpu.VMEM((ROWS, WIDTH), F32),
            edges,
            edges,
            edges,
            pltpu.VMEM((NBLOCK, 8, BLK), F32),
            pltpu.VMEM((NBLOCK, HPAD, BLK), F32),
            pltpu.VMEM((NBLOCK, HPAD, BLK), BF16),
            pltpu.VMEM((NBLOCK, BLK, HPAD), F32),
            pltpu.VMEM((N_SRC * N_SRC, HARM, 2 * TRIP), BF16),
            pltpu.VMEM((NBLOCK, HPAD, 4 * TRIP), BF16),
            pltpu.VMEM((NBLOCK, HPAD, WIDTH), BF16),
            pltpu.VMEM((N_SRC, ATOM_ROWS, CHUNK), BF16),
            pltpu.VMEM((NBLOCK, BLK, BLK), BF16),
            pltpu.VMEM((NBLOCK, BLK, 2 * ATOM_ROWS), BF16),
            pltpu.VMEM(down.shape, BF16),
            pltpu.VMEM(trip_w.shape, BF16),
            pltpu.VMEM(edge_w.shape, BF16),
            pltpu.VMEM((ATOM_ROWS, WIDTH), F32),
            pltpu.VMEM((HALVES, N_SRC, PIECE, WIDTH), BF16),
            pltpu.VMEM((HALVES, N_SRC, PIECE, WIDTH), BF16),
            pltpu.VMEM((HALVES, PIECE, WIDTH), BF16),
            pltpu.VMEM((HALVES, 2, N_SRC, PIECE, WIDTH), BF16),
            dma((4,)),
            dma,
            dma((N_SRC,)),
            dma,
            dma((N_SRC,)),
            dma,
            dma((HALVES,)),
            dma((HALVES,)),
            dma((HALVES,)),
        ],
        compiler_params=pltpu.CompilerParams(
            collective_id=0, has_side_effects=True, vmem_limit_bytes=60 << 20
        ),
    )(
        triplets.T,
        directions,
        src_atom.reshape(NBLOCK, BLK),
        dst_atom.reshape(NBLOCK, BLK),
        rev_pos.reshape(NBLOCK, BLK),
        counts,
        edge_state.reshape(DEVS, CAP, WIDTH),
        down,
        trip_w,
        edge_w,
    )
    return out.reshape(ROWS, WIDTH)


def solution(mesh):
    placed = (
        P(("src", "dst"), None),
        P(None, ("src", "dst")),
        P(("src", "dst")),
        P(("src", "dst")),
        P(("src", "dst")),
        P(("src", "dst"), None),
        P(("src", "dst"), None),
        P(),
        P(),
        P(),
    )
    return jax.shard_map(
        body, mesh=mesh, in_specs=placed, out_specs=P(("src", "dst"), None), check_vma=False
    )
```
